128 devices in a mesh: row: 32 (over y_lo, z, x), col: 4 (over y_hi, core).
Axes of the slice: x: 4, y: 4 (y_hi: 2, y_lo: 2; y = y_hi * 2 + y_lo), z: 4, core: 2. Of those that a mesh axis runs over, the one named last changes fastest.
Arguments:
- flow: bfloat16 [8192, 8192], P('row', 'col'), may hold values from 0.0009994507 to 1
- pattern: int32 [32, 32], P('row', 'col'), may hold values 0 or 1
- keep: int32 [32, 32], P('row', 'col'), may hold values 0 or 1
Outputs:
- clustered: float32 [8192, 8192], P('row', 'col')
The draws below stay inside these ranges and needn't reach their ends.
All inputs are finite; a program needn't handle non-finite values. No bound on the sum of `pattern` or of `keep` on one device may be relied on, other than what follows from the above.
Results may differ from the reference program's by a relative error of at most 0.00046.
Values may be sent and summed in bfloat16 or wider, within the bound.
A program may use at most 128 MiB of HBM per device.

```python
import math
import jax
import jax.numpy as jnp

TILE = 256
NT = 32
ORDER = 8192


def touch_ends(entries, key, low, high):
    index_at = [jax.random.randint(jax.random.fold_in(key, axis), (), 0, length) for axis, length in enumerate(entries.shape)]
    main_axis = entries.shape.index(max(entries.shape))
    beside = index_at[:main_axis] + [(index_at[main_axis] + 1) % entries.shape[main_axis]] + index_at[main_axis + 1:]
    return entries.at[tuple(index_at)].set(low).at[tuple(beside)].set(high)


def block_levels(rng, shape, split, least, top_value):
    level = 1.0
    for position, parts in split:
        draws = jax.random.uniform(jax.random.fold_in(jax.random.fold_in(rng, 6), position), (parts,), jnp.float32, least / len(split), top_value / len(split))
        level = level * jnp.repeat(jnp.exp(draws), shape[position] // parts).reshape((-1,) + (1,) * (len(shape) - 1 - position))
    return level


def setup_inputs(seed: int = 0) -> dict:
    key_list = jax.random.split(jax.random.key(seed), 4)
    return {
        "flow": jnp.clip(jnp.exp(math.log(1.0) - 6.9083047 * jax.random.uniform(key_list[0], (ORDER, ORDER), jnp.float32) ** block_levels(key_list[0], (ORDER, ORDER), ((0, 32), (1, 4)), -0.2, 0.2)), 0.0009994507, 1.0).astype(jnp.bfloat16),
        "pattern": touch_ends((jax.random.randint(key_list[1], (NT, NT), 0, 5) < 3).astype(jnp.int32), jax.random.fold_in(key_list[1], 1), 0, 1),
        "keep": touch_ends((jax.random.randint(key_list[2], (NT, NT), 0, 5) < 4).astype(jnp.int32), jax.random.fold_in(key_list[2], 1), 0, 1),
    }


def tile_mask(grid, tile):
    count = grid.shape[0]
    wide = jnp.broadcast_to(grid[:, None, :, None], (count, tile, count, tile))
    return wide.reshape(count * tile, count * tile)


def reference(flow, pattern, keep):
    order = ORDER
    loops = jnp.eye(order, dtype=jnp.float32)
    base = flow.astype(jnp.float32) * tile_mask((pattern > 0).astype(jnp.float32), TILE) + loops
    mass = jnp.sum(base, axis=0)
    stochastic = (base / mass[None, :]).astype(jnp.bfloat16)
    expanded = jnp.dot(stochastic, stochastic, preferred_element_type=jnp.float32)
    kept = jnp.logical_or(keep > 0, jnp.eye(NT, dtype=jnp.int32) > 0).astype(jnp.float32)
    expanded = expanded * tile_mask(kept, TILE)
    inflated = expanded * expanded
    totals = jnp.sum(inflated, axis=0)
    scale = order / totals
    return inflated * scale[None, :]
```

```python
import jax
import jax.numpy as jnp
from jax import lax
from jax.experimental import pallas as pl
from jax.experimental.pallas import tpu as pltpu
from jax.sharding import PartitionSpec as P

MESH = pl.DeviceIdType.MESH
F32 = jnp.float32
BF16 = jnp.bfloat16


class Place:
    def __init__(self):
        row, col = lax.axis_index("row"), lax.axis_index("col")
        self.row, self.col = row, col
        self.yl, self.z, self.x = row // 16, (row // 4) % 4, row % 4
        self.yh, self.c = col // 2, col % 2

    def dev(self, x=None, z=None, yl=None, yh=None, c=None):
        x = self.x if x is None else x
        z = self.z if z is None else z
        yl = self.yl if yl is None else yl
        yh = self.yh if yh is None else yh
        c = self.c if c is None else c
        return (yl * 16 + z * 4 + x, yh * 2 + c)


class Copies:
    def __init__(self, send_sem, recv_sem, me):
        self.send_sem, self.recv_sem, self.me = send_sem, recv_sem, me
        self.ids, self.sent = {}, []

    def slot(self, name):
        return self.ids.setdefault(name, len(self.ids))

    def make(self, name, src, dst, dev):
        k = self.slot(name)
        return pltpu.make_async_remote_copy(
            src_ref=src, dst_ref=dst, send_sem=self.send_sem.at[k], recv_sem=self.recv_sem.at[k],
            device_id=dev, device_id_type=MESH)

    def send(self, name, src, dst, dev):
        copy = self.make(name, src, dst, dev)
        copy.start()
        self.sent.append(copy)

    def wait(self, name, landed, dev):
        self.make(name, landed, landed, dev).wait_recv()

    def drain(self):
        for copy in self.sent:
            copy.wait_send()


def greet(devices):
    barrier = pltpu.get_barrier_semaphore()
    for dev in devices:
        pl.semaphore_signal(barrier, inc=1, device_id=dev, device_id_type=MESH)
    pl.semaphore_wait(barrier, len(devices))


def normalise_kernel(tile, flow, pattern, keep, s_out, km_out, xs, zs, kx, km, send_sem, recv_sem, local_sem):
    me = Place()
    rows, cols = flow.shape
    nt = cols // tile
    wide = cols // 4
    others = [(dz, dy) for dy in (0, 1) for dz in range(4) if (dz, dy) != (0, 0)]
    net = Copies(send_sem, recv_sem, me)
    greet([me.dev(x=(me.x + d) % 4) for d in (1, 2, 3)]
          + [me.dev(z=(me.z + dz) % 4, yl=(me.yl + dy) % 2) for dz, dy in others])

    def base(t):
        on = (pattern[0, t] > 0).astype(F32)
        block = flow[:, t * tile:(t + 1) * tile].astype(F32) * on
        r = lax.broadcasted_iota(jnp.int32, (rows, tile), 0) + me.row * rows
        k = lax.broadcasted_iota(jnp.int32, (rows, tile), 1) + (me.col * cols + t * tile)
        return block + (r == k).astype(F32)

    for t in range(nt):
        xs[me.x, :, t * tile:(t + 1) * tile] = jnp.sum(base(t), axis=0, keepdims=True)
    for d in (1, 3, 2):
        net.send(("x", d), xs.at[me.x], xs.at[me.x], me.dev(x=(me.x + d) % 4))
    for t in range(nt):
        kept = jnp.logical_or(keep[0, t] > 0, me.row == me.col * nt + t).astype(F32)
        kx[:, t * tile:(t + 1) * tile] = jnp.broadcast_to(kept, (8, tile))
    chunk = lambda j: kx.at[:, pl.ds(pl.multiple_of(j * wide, wide), wide)]
    for d in (1, 3, 2):
        to = (me.z + d) % 4
        net.send(("k", d), chunk(to), km.at[me.z], me.dev(z=to))
    own = pltpu.make_async_copy(chunk(me.z), km.at[me.z], local_sem)
    own.start()
    for d in (1, 3, 2):
        src = (me.x - d + 4) % 4
        net.wait(("x", d), xs.at[src], me.dev(x=src))
    here = me.yl * 4 + me.z
    zs[here] = xs[0] + xs[1] + xs[2] + xs[3]
    for dz, dy in others:
        net.send(("z", dz, dy), zs.at[here], zs.at[here], me.dev(z=(me.z + dz) % 4, yl=(me.yl + dy) % 2))
    for dz, dy in others:
        z, yl = (me.z - dz + 4) % 4, (me.yl + dy) % 2
        net.wait(("z", dz, dy), zs.at[yl * 4 + z], me.dev(z=z, yl=yl))
    mass = ((zs[0] + zs[1]) + (zs[2] + zs[3])) + ((zs[4] + zs[5]) + (zs[6] + zs[7]))
    inverse = 1.0 / mass
    for t in range(nt):
        s_out[:, t * tile:(t + 1) * tile] = (base(t) * inverse[:, t * tile:(t + 1) * tile]).astype(BF16)
    own.wait()
    for d in (1, 3, 2):
        src = (me.z - d + 4) % 4
        net.wait(("k", d), km.at[src], me.dev(z=src))
    km_out[...] = km[...]
    net.drain()


def product_kernel(s, km, out, scale_out, a, b, relay, c, ts, sc, send_sem, recv_sem, local_sem):
    me = Place()
    rows, cols = s.shape
    half = rows // 2
    wide = cols // 4
    x, z, yl, yh, core = me.x, me.z, me.yl, me.yh, me.c
    y = yh * 2 + yl
    net = Copies(send_sem, recv_sem, me)
    zp, zm, z2 = (z + 1) % 4, (z + 3) % 4, (z + 2) % 4
    xp, xm, x2 = (x + 1) % 4, (x + 3) % 4, (x + 2) % 4
    turn = 1 + 2 * core
    yn, ys = (y + turn) % 4, (y + 4 - turn) % 4
    group = [(dx, dy) for dy in (0, 1) for dx in range(4) if (dx, dy) != (0, 0)]
    mate = me.dev(c=1 - core)
    to_y = me.dev(yl=yn % 2, yh=yn // 2)
    from_y = me.dev(yl=ys % 2, yh=ys // 2)
    greet([me.dev(z=zp), me.dev(z=zm), me.dev(z=z2), to_y, from_y, mate]
          + [me.dev(x=(x + dx) % 4, yl=(yl + dy) % 2) for dx, dy in group])

    q0, q1 = yh * 2 + core, (1 - yh) * 2 + core
    q_of = (q0, q1)

    def a_at(q, zz, h=None):
        if h is None:
            return a.at[q, pl.ds(pl.multiple_of(zz * rows, rows), rows)]
        return a.at[q, pl.ds(pl.multiple_of(zz * rows + h * half, half), half)]

    def b_at(yy, zz, xx, h=None):
        start = (yy * 16 + zz * 4 + xx) * rows
        if h is None:
            return b.at[pl.ds(pl.multiple_of(start, rows), rows)]
        return b.at[pl.ds(pl.multiple_of(start + h * half, half), half)]

    def s_chunk(j):
        return s.at[:, pl.ds(pl.multiple_of(j * wide, wide), wide)]

    def s_half(h):
        return s.at[pl.ds(h * half, half)]

    z_order = (z, zp, zm, z2)
    pieces = [(yl, zz) for zz in z_order] + [(1 - yl, zz) for zz in z_order]

    def spread_x(i, src):
        yy, zz = pieces[i]
        net.send(("bx+", i), src, b_at(yy, zz, x), me.dev(x=xp))
        net.send(("bx-", i), src, b_at(yy, zz, x), me.dev(x=xm))

    def forward_x(i):
        yy, zz = pieces[i]
        net.wait(("bx+", i), b_at(yy, zz, xm), me.dev(x=xm))
        net.send(("bf+", i), b_at(yy, zz, xm, 0), b_at(yy, zz, xm, 0), me.dev(x=xp))
        net.wait(("bx-", i), b_at(yy, zz, xp), me.dev(x=xp))
        net.send(("bf-", i), b_at(yy, zz, xp, 1), b_at(yy, zz, xp, 1), me.dev(x=xm))

    def last_x(i):
        yy, zz = pieces[i]
        net.wait(("bf+", i), b_at(yy, zz, x2, 0), me.dev(x=xm))
        net.wait(("bf-", i), b_at(yy, zz, x2, 1), me.dev(x=xp))

    def cross_y(i, src):
        yy, zz = pieces[i]
        net.send(("by", i), src, b_at(yy, zz, x), me.dev(yl=1 - yl))

    def home(i):
        yy, zz = pieces[i]
        if i < 4:
            name, src = {1: ("bz-", zp), 2: ("bz+", zm), 3: ("bz2", z2)}[i]
            net.wait(name, b_at(yl, zz, x), me.dev(z=src))
            spread_x(i, b_at(yl, zz, x))
            cross_y(i, b_at(yl, zz, x))
        else:
            net.wait(("by", i - 4), b_at(yy, zz, x), me.dev(yl=1 - yl))
            spread_x(i, b_at(yy, zz, x))

    def to_mate(p, k, h, src):
        zz = (z, zm, zp, z2)[k]
        net.send(("ac", p, k, h), src, a_at(q_of[p], zz, h), mate)

    def z_ring(p, src):
        for first in (0, 1):
            h = first
            net.send(("az+", p, h), src(h), a_at(q_of[p], z, h), me.dev(z=zp))
            h = 1 - first
            net.send(("az-", p, h), src(h), a_at(q_of[p], z, h), me.dev(z=zm))

    def z_take(p, k, h):
        q = q_of[p]
        if k == 1:
            net.wait(("az+", p, h), a_at(q, zm, h), me.dev(z=zm))
            if h == 0:
                net.send(("af+", p), a_at(q, zm, 0), a_at(q, zm, 0), me.dev(z=zp))
            to_mate(p, 1, h, a_at(q, zm, h))
        elif k == 2:
            net.wait(("az-", p, h), a_at(q, zp, h), me.dev(z=zp))
            if h == 1:
                net.send(("af-", p), a_at(q, zp, 1), a_at(q, zp, 1), me.dev(z=zm))
            to_mate(p, 2, h, a_at(q, zp, h))
        else:
            net.wait(("af+", p) if h == 0 else ("af-", p), a_at(q, z2, h), me.dev(z=zm if h == 0 else zp))
            to_mate(p, 3, h, a_at(q, z2, h))

    net.send("bz+", s_chunk(zp), b_at(yl, z, x), me.dev(z=zp))
    net.send("bz-", s_chunk(zm), b_at(yl, z, x), me.dev(z=zm))
    net.send("bz2", s_chunk(z2), b_at(yl, z, x), me.dev(z=z2))
    spread_x(0, s_chunk(z))
    cross_y(0, s_chunk(z))
    z_ring(0, s_half)
    for h in (0, 1):
        net.send(("ay1", h), s_half(h), relay.at[pl.ds(h * half, half)], to_y)
    for h in (0, 1):
        to_mate(0, 0, h, s_half(h))
    local = [pltpu.make_async_copy(s_chunk(z), b_at(yl, z, x), local_sem.at[0]),
             pltpu.make_async_copy(s, a_at(q0, z), local_sem.at[1])]
    for copy in local:
        copy.start()

    def relay_y(h):
        part = relay.at[pl.ds(h * half, half)]
        net.wait(("ay1", h), part, from_y)
        net.send(("ay2", h), part, a_at((ys // 2) * 2 + core, z, h), to_y)

    def take_y(h):
        net.wait(("ay2", h), a_at(q1, z, h), from_y)
        src = lambda k: a_at(q1, z, k)
        net.send(("az+", 1, h), src(h), src(h), me.dev(z=zp))
        net.send(("az-", 1, h), src(h), src(h), me.dev(z=zm))
        to_mate(1, 0, h, src(h))

    home(1)
    home(2)
    forward_x(0)
    relay_y(0)
    home(3)
    forward_x(1)
    home(4)
    z_take(0, 1, 0)
    z_take(0, 2, 1)
    relay_y(1)
    forward_x(2)
    home(5)
    z_take(0, 1, 1)
    z_take(0, 2, 0)
    take_y(0)
    forward_x(3)
    home(6)
    take_y(1)
    z_take(0, 3, 0)
    z_take(0, 3, 1)
    forward_x(4)
    home(7)
    z_take(1, 1, 0)
    z_take(1, 2, 0)
    forward_x(5)
    forward_x(6)
    z_take(1, 1, 1)
    z_take(1, 2, 1)
    forward_x(7)
    for i in range(8):
        last_x(i)
    for copy in local:
        copy.wait()

    def mate_ready(p):
        q = (yh if p == 0 else 1 - yh) * 2 + 1 - core
        for k, zz in enumerate((z, zm, zp, z2)):
            for h in (0, 1):
                net.wait(("ac", p, k, h), a_at(q, zz, h), mate)

    def part(q, zz, n):
        left = a[q, pl.ds(pl.multiple_of(zz * rows, rows), rows)]
        right = b[pl.ds(pl.multiple_of(q * cols, cols), cols), pl.ds(pl.multiple_of(n * 256, 256), 256)]
        return jnp.dot(left, right, preferred_element_type=F32)

    def early(step, _):
        zz, n = step // 2, step % 2
        at = pl.ds(pl.multiple_of(n * 256, 256), 256)
        c[zz, :, at] = part(yh * 2, zz, n) + part(yh * 2 + 1, zz, n)
        return _

    mate_ready(0)
    lax.fori_loop(0, 8, early, 0)
    z_take(1, 3, 0)
    z_take(1, 3, 1)
    mate_ready(1)
    ts[yl * 4 + x] = jnp.zeros(ts.shape[1:], F32)
    for k, (zz, d) in enumerate(((z2, 2), (zp, 1), (zm, 3), (z, 0))):
        def late(n, _, zz=zz):
            at = pl.ds(pl.multiple_of(n * 256, 256), 256)
            full = c[zz, :, at] + part((1 - yh) * 2, zz, n) + part((1 - yh) * 2 + 1, zz, n)
            full = full * km[zz, 0:1, at]
            full = full * full
            c[zz, :, at] = full
            ts[yl * 4 + x, :, at] += jnp.sum(full, axis=0, keepdims=True)
            return _

        lax.fori_loop(0, 2, late, 0)
        mine = out.at[:, pl.ds(pl.multiple_of(z * wide, wide), wide)]
        if d:
            net.send(("c", d), c.at[zz], mine, me.dev(z=(z + d) % 4))
        else:
            keep = pltpu.make_async_copy(c.at[zz], mine, local_sem.at[2])
            keep.start()
    for dx, dy in group:
        net.send(("t", dx, dy), ts.at[yl * 4 + x], ts.at[yl * 4 + x], me.dev(x=(x + dx) % 4, yl=(yl + dy) % 2))
    for dx, dy in group:
        xx, yy = (x - dx + 4) % 4, (yl + dy) % 2
        net.wait(("t", dx, dy), ts.at[yy * 4 + xx], me.dev(x=xx, yl=yy))
    total = ((ts[0] + ts[1]) + (ts[2] + ts[3])) + ((ts[4] + ts[5]) + (ts[6] + ts[7]))
    sc[z] = (rows * 32) / total
    for d in (1, 3, 2):
        net.send(("s", d), sc.at[z], sc.at[z], me.dev(z=(z + d) % 4))
    keep.wait()
    for d in (1, 3, 2):
        src = (z - d + 4) % 4
        net.wait(("s", d), sc.at[src], me.dev(z=src))
    scale_out[...] = sc[...]
    for d in (1, 3, 2):
        src = (z - d + 4) % 4
        net.wait(("c", d), out.at[:, pl.ds(pl.multiple_of(src * wide, wide), wide)], me.dev(z=src))
    net.drain()


def body(flow, pattern, keep):
    rows, cols = flow.shape
    nt = pattern.shape[1]
    tile = cols // nt
    wide = cols // 4
    vmem = pl.BlockSpec(memory_space=pltpu.VMEM)
    smem = pl.BlockSpec(memory_space=pltpu.SMEM)
    anyspace = pl.BlockSpec(memory_space=pl.ANY)
    s, km = pl.pallas_call(
        lambda *refs: normalise_kernel(tile, *refs),
        out_shape=(jax.ShapeDtypeStruct((rows, cols), BF16), jax.ShapeDtypeStruct((4, 8, wide), F32)),
        in_specs=[vmem, smem, smem],
        out_specs=(vmem, vmem),
        scratch_shapes=[
            pltpu.VMEM((4, 1, cols), F32),
            pltpu.VMEM((8, 1, cols), F32),
            pltpu.VMEM((8, cols), F32),
            pltpu.VMEM((4, 8, wide), F32),
            pltpu.SemaphoreType.DMA((13,)),
            pltpu.SemaphoreType.DMA((13,)),
            pltpu.SemaphoreType.DMA,
        ],
        compiler_params=pltpu.CompilerParams(collective_id=0, has_side_effects=True),
        name="normalise",
    )(flow, pattern, keep)
    messages = 92
    inflated, scale = pl.pallas_call(
        product_kernel,
        out_shape=(jax.ShapeDtypeStruct((rows, cols), F32), jax.ShapeDtypeStruct((4, 1, wide), F32)),
        in_specs=[anyspace, vmem],
        out_specs=(anyspace, vmem),
        scratch_shapes=[
            pltpu.VMEM((4, 4 * rows, cols), BF16),
            pltpu.VMEM((32 * rows, wide), BF16),
            pltpu.VMEM((rows, cols), BF16),
            pltpu.VMEM((4, rows, wide), F32),
            pltpu.VMEM((8, 1, wide), F32),
            pltpu.VMEM((4, 1, wide), F32),
            pltpu.SemaphoreType.DMA((messages,)),
            pltpu.SemaphoreType.DMA((messages,)),
            pltpu.SemaphoreType.DMA((3,)),
        ],
        compiler_params=pltpu.CompilerParams(
            collective_id=1, has_side_effects=True, vmem_limit_bytes=48 * 1024 * 1024),
        name="product",
    )(s, km)
    return inflated * scale.reshape(1, cols)


def solution(mesh):
    return jax.shard_map(
        body,
        mesh=mesh,
        in_specs=(P("row", "col"), P("row", "col"), P("row", "col")),
        out_specs=P("row", "col"),
        check_vma=False,
    )
```

```python
import jax
import jax.numpy as jnp
from jax import lax
from jax.experimental import pallas as pl
from jax.experimental.pallas import tpu as pltpu
from jax.sharding import PartitionSpec as P

MESH = pl.DeviceIdType.MESH
F32 = jnp.float32
BF16 = jnp.bfloat16


class Place:
    def __init__(self):
        row, col = lax.axis_index("row"), lax.axis_index("col")
        self.row, self.col = row, col
        self.yl, self.z, self.x = row // 16, (row // 4) % 4, row % 4
        self.yh, self.c = col // 2, col % 2

    def dev(self, x=None, z=None, yl=None, yh=None, c=None):
        x = self.x if x is None else x
        z = self.z if z is None else z
        yl = self.yl if yl is None else yl
        yh = self.yh if yh is None else yh
        c = self.c if c is None else c
        return (yl * 16 + z * 4 + x, yh * 2 + c)


class Copies:
    def __init__(self, send_sem, recv_sem, me):
        self.send_sem, self.recv_sem, self.me = send_sem, recv_sem, me
        self.ids, self.sent = {}, []

    def slot(self, name):
        return self.ids.setdefault(name, len(self.ids))

    def make(self, name, src, dst, dev):
        k = self.slot(name)
        return pltpu.make_async_remote_copy(
            src_ref=src, dst_ref=dst, send_sem=self.send_sem.at[k], recv_sem=self.recv_sem.at[k],
            device_id=dev, device_id_type=MESH)

    def send(self, name, src, dst, dev):
        copy = self.make(name, src, dst, dev)
        copy.start()
        self.sent.append(copy)

    def wait(self, name, landed, dev):
        self.make(name, landed, landed, dev).wait_recv()

    def drain(self):
        for copy in self.sent:
            copy.wait_send()


def kernel(tile, flow, pattern, keep, q_out, gs_out, a, b, m, araw, braw, xraw, c, cq, xs, zs, inv, kx, km, ts, gsend, gs,
           send_sem, recv_sem, local_sem):
    me = Place()
    rows, cols = flow.shape
    nt = cols // tile
    half = rows // 2
    wide = cols // 4
    ring = 3 * rows // 4
    parts = ((0, ring // 2), (ring // 2, ring // 2), (ring, rows - ring))
    x, z, yl, yh, core = me.x, me.z, me.yl, me.yh, me.c
    net = Copies(send_sem, recv_sem, me)
    zp, zm, z2 = (z + 1) % 4, (z + 3) % 4, (z + 2) % 4
    xp, xm, x2 = (x + 1) % 4, (x + 3) % 4, (x + 2) % 4
    around = [(d, dy) for dy in (0, 1) for d in range(4) if (d, dy) != (0, 0)]
    mate, across, beside = me.dev(c=1 - core), me.dev(yh=1 - yh), me.dev(yl=1 - yl)
    barrier = pltpu.get_barrier_semaphore()
    peers = ([me.dev(x=(x + d) % 4, yl=(yl + dy) % 2) for d, dy in around]
             + [me.dev(z=(z + d) % 4, yl=(yl + dy) % 2) for d, dy in around if d] + [mate, across])
    for dev in peers:
        pl.semaphore_signal(barrier, inc=1, device_id=dev, device_id_type=MESH)

    q0, q1 = yh * 2 + core, (1 - yh) * 2 + core
    q_of = (q0, q1)

    def block(yy, zz, xx):
        return yy * 16 + zz * 4 + xx

    def a_at(q, zz, start=0, size=rows):
        return a.at[q, pl.ds(pl.multiple_of(zz * rows + start, 32), size)]

    def b_at(yy, zz, xx, start=0, size=rows):
        return b.at[pl.ds(pl.multiple_of(block(yy, zz, xx) * rows + start, half), size)]

    def chunk(ref, j):
        return ref.at[:, pl.ds(pl.multiple_of(j * wide, wide), wide)]

    def eye(first_row, first_col):
        r = lax.broadcasted_iota(jnp.int32, (rows, tile), 0)
        k = lax.broadcasted_iota(jnp.int32, (rows, tile), 1)
        return (r - k == first_col - first_row).astype(F32)

    for t in range(nt):
        at = slice(t * tile, (t + 1) * tile)
        on = (pattern[0, t] > 0).astype(F32)
        masked = flow[:, at].astype(F32) * on
        m[:, at] = masked.astype(BF16)
        masked = masked + eye(me.row * rows, me.col * cols + t * tile)
        xs[x, :, at] = jnp.sum(masked, axis=0, keepdims=True)
        kept = jnp.logical_or(keep[0, t] > 0, me.row == me.col * nt + t).astype(F32)
        kx[:, at] = jnp.broadcast_to(kept, (8, tile))
    km[z] = kx[:, pl.ds(pl.multiple_of(z * wide, wide), wide)]
    pl.semaphore_wait(barrier, len(peers))

    for d in (1, 3, 2):
        net.send(("mx", d), xs.at[x], xs.at[x], me.dev(x=(x + d) % 4))
    net.send("bz+", chunk(m, zp), braw.at[0], me.dev(z=zp))
    net.send("bz-", chunk(m, zm), braw.at[1], me.dev(z=zm))
    net.send(("bx+", 0), chunk(m, z), xraw.at[0], me.dev(x=xp))
    net.send(("bx-", 0), chunk(m, z), xraw.at[1], me.dev(x=xm))
    for d in (1, 3, 2):
        src = (x - d + 4) % 4
        net.wait(("mx", d), xs.at[src], me.dev(x=src))
    here = yl * 4 + z
    zs[here] = (xs[0] + xs[1]) + (xs[2] + xs[3])
    for d, dy in around:
        net.send(("mz", d, dy), zs.at[here], zs.at[here], me.dev(z=(z + d) % 4, yl=(yl + dy) % 2))
    net.send("bz2", chunk(m, z2), braw.at[2], me.dev(z=z2))
    for d in (1, 3, 2):
        net.send(("k", d), chunk(kx, (z + d) % 4), km.at[z], me.dev(z=(z + d) % 4))
    for first in (0, 1):
        for name, h, k, to in (("az0+", first, 0, zp), ("az0-", 1 - first, 1, zm)):
            at = pl.ds(h * half, half)
            net.send((name, h), m.at[at], araw.at[k, at], me.dev(z=to))

    z_order = (z, zp, zm, z2)
    pieces = [(yl, zz) for zz in z_order] + [(1 - yl, zz) for zz in z_order]

    def landed_x(i, k, start=0, size=rows):
        if i == 0:
            return xraw.at[k, pl.ds(start, size)]
        yy, zz = pieces[i]
        return b_at(yy, zz, (xm, xp, x2)[k], start, size)

    def sent_x(i, k, start=0, size=rows):
        if i == 0:
            return xraw.at[k, pl.ds(start, size)]
        yy, zz = pieces[i]
        return b_at(yy, zz, x if k < 2 else (xm if start == 0 else xp), start, size)

    def spread_x(i, src):
        net.send(("bx+", i), src, sent_x(i, 0), me.dev(x=xp))
        net.send(("bx-", i), src, sent_x(i, 1), me.dev(x=xm))

    def forward_x(i):
        net.wait(("bx+", i), landed_x(i, 0), me.dev(x=xm))
        net.send(("bf+", i), landed_x(i, 0, 0, half), sent_x(i, 2, 0, half), me.dev(x=xp))
        net.wait(("bx-", i), landed_x(i, 1), me.dev(x=xp))
        net.send(("bf-", i), landed_x(i, 1, half, half), sent_x(i, 2, half, half), me.dev(x=xm))

    def last_x(i):
        net.wait(("bf+", i), landed_x(i, 2, 0, half), me.dev(x=xm))
        net.wait(("bf-", i), landed_x(i, 2, half, half), me.dev(x=xp))

    forward_x(0)

    for d, dy in around:
        zz, yy = (z - d + 4) % 4, (yl + dy) % 2
        net.wait(("mz", d, dy), zs.at[yy * 4 + zz], me.dev(z=zz, yl=yy))
    mass = ((zs[0] + zs[1]) + (zs[2] + zs[3])) + ((zs[4] + zs[5]) + (zs[6] + zs[7]))
    inv[...] = 1.0 / mass

    def normalise(dst, src, count, first_row, first_tile):
        def step(t, _):
            at = pl.ds(pl.multiple_of(t * tile, tile), tile)
            there = pl.ds(pl.multiple_of((first_tile + t) * tile, tile), tile)
            value = src[:, at].astype(F32) + eye(first_row, me.col * cols + (first_tile + t) * tile)
            dst[:, at] = (value * inv[:, there]).astype(BF16)
            return _

        lax.fori_loop(0, count, step, 0)

    def normalise_b(dst_x, zz, src):
        normalise(b_at(yl, zz, dst_x), src, wide // tile, block(yl, zz, dst_x) * rows, z * (wide // tile))

    def normalise_a(zz, src):
        normalise(a_at(q0, zz), src, nt, block(yl, zz, x) * rows, 0)

    def home(i):
        yy, zz = pieces[i]
        piece = b_at(yy, zz, x)
        if i < 4:
            name, k, src = {1: ("bz-", 1, zp), 2: ("bz+", 0, zm), 3: ("bz2", 2, z2)}[i]
            net.wait(name, braw.at[k], me.dev(z=src))
            normalise_b(x, zz, braw.at[k])
            spread_x(i, piece)
            net.send(("by", i), piece, piece, beside)
        else:
            net.wait(("by", i - 4), piece, beside)
            spread_x(i, piece)

    def take_z0(k, h):
        at = pl.ds(h * half, half)
        if k == 0:
            net.wait(("az0+", h), araw.at[0, at], me.dev(z=zm))
            if h == 0:
                net.send("af0+", araw.at[0, at], araw.at[2, at], me.dev(z=zp))
        elif k == 1:
            net.wait(("az0-", h), araw.at[1, at], me.dev(z=zp))
            if h == 1:
                net.send("af0-", araw.at[1, at], araw.at[2, at], me.dev(z=zm))
        elif h == 0:
            net.wait("af0+", araw.at[2, at], me.dev(z=zm))
        else:
            net.wait("af0-", araw.at[2, at], me.dev(z=zp))

    def finish_z0(k):
        zz = (zm, zp, z2)[k]
        normalise_a(zz, araw.at[k])
        net.send(("ac0", k + 1), a_at(q0, zz), a_at(q0, zz), mate)
        start, size = parts[2]
        net.send(("ar", k), a_at(q0, zz, start, size), a_at(q0, zz, start, size), across)

    def to_mate(k, p):
        zz = (z, zm, zp, z2)[k]
        net.send(("ac1", k, p), a_at(q1, zz, *parts[p]), a_at(q1, zz, *parts[p]), mate)

    def take_y(p):
        at = a_at(q1, z, *parts[p])
        net.wait(("ay", p), at, across)
        if p < 2:
            net.send(("az1+", p), at, at, me.dev(z=zp))
            net.send(("az1-", p), at, at, me.dev(z=zm))
        to_mate(0, p)

    def take_rest(k):
        net.wait(("ar", k), a_at(q1, (zm, zp, z2)[k], *parts[2]), across)
        to_mate(k + 1, 2)

    def take_z1(k, p):
        at = a_at(q1, (zm, zp, z2)[k], *parts[p])
        if k == 0:
            net.wait(("az1+", p), at, me.dev(z=zm))
            if p == 0:
                net.send("af1+", at, at, me.dev(z=zp))
        elif k == 1:
            net.wait(("az1-", p), at, me.dev(z=zp))
            if p == 1:
                net.send("af1-", at, at, me.dev(z=zm))
        elif p == 0:
            net.wait("af1+", at, me.dev(z=zm))
        else:
            net.wait("af1-", at, me.dev(z=zp))
        to_mate(k + 1, p)

    def mate0(k):
        at = a_at(yh * 2 + 1 - core, (z, zm, zp, z2)[k])
        net.wait(("ac0", k), at, mate)

    def mate1(k, ps=(0, 1, 2)):
        for p in ps:
            net.wait(("ac1", k, p), a_at((1 - yh) * 2 + 1 - core, (z, zm, zp, z2)[k], *parts[p]), mate)

    def units(yy, piece, ks, first=False):
        zi = z_order[piece]
        deep = 4 * rows
        left_at = pl.ds(pl.multiple_of((zi % 2) * deep, deep), deep)
        right_at = pl.ds(pl.multiple_of((yy * 4 + zi) * deep, deep), deep)
        q = yy * 2 + zi // 2

        def step(j, _):
            k, n = j // 2, j % 2
            zz = (z + (ks[0] if len(ks) == 1 else k if len(ks) == 4 else ks[0] + 2 * k)) % 4
            at = pl.ds(pl.multiple_of(n * 256, 256), 256)
            left = a[q, pl.ds(pl.multiple_of(zz * rows, rows), rows), left_at]
            value = jnp.dot(left, b[right_at, at], preferred_element_type=F32)
            c[zz, :, at] = value if first else c[zz, :, at] + value
            return _

        lax.fori_loop(0, 2 * len(ks), step, 0)

    home(1)
    normalise_b(x, z, chunk(m, z))
    net.send(("by", 0), b_at(yl, z, x), b_at(yl, z, x), beside)
    home(2)
    normalise_a(z, m)
    for p in (0, 1, 2):
        at = a_at(q0, z, *parts[p])
        net.send(("ay", p), at, at, across)
    net.send(("ac0", 0), a_at(q0, z), a_at(q0, z), mate)
    home(3)
    forward_x(1)
    home(4)
    last_x(0)
    for k, xx in enumerate((xm, xp, x2)):
        normalise_b(xx, z, xraw.at[k])
    take_z0(0, 0)
    take_z0(1, 1)
    forward_x(2)
    home(5)
    take_y(0)
    forward_x(3)
    take_z0(0, 1)
    take_z0(1, 0)
    finish_z0(0)
    finish_z0(1)
    take_y(1)
    take_y(2)
    home(6)
    forward_x(4)
    take_z0(2, 0)
    take_z0(2, 1)
    finish_z0(2)
    home(7)
    forward_x(5)
    for i in (1, 2, 3):
        last_x(i)
    for k in range(4):
        mate0(k)
    mate1(0)
    last_x(4)
    take_rest(0)
    take_rest(1)
    units(yh, 0, (0, 1, 2, 3), first=True)
    forward_x(6)
    last_x(5)
    take_z1(0, 0)
    take_z1(1, 1)
    units(yh, 1, (0, 1, 2, 3))
    units(1 - yh, 0, (0,))
    units(1 - yh, 1, (0,))
    take_rest(2)
    take_z1(0, 1)
    take_z1(1, 0)
    last_x(6)
    units(yh, 2, (0, 1, 2, 3))
    forward_x(7)
    mate1(1)
    mate1(2)
    units(1 - yh, 2, (0,))
    for piece in (0, 1, 2):
        units(1 - yh, piece, (1, 3))
    take_z1(2, 0)
    take_z1(2, 1)
    last_x(7)
    units(yh, 3, (0, 1, 2, 3))
    units(1 - yh, 3, (1, 3))
    mine = yl * 4 + x
    for d in (1, 3, 2):
        src = (z - d + 4) % 4
        net.wait(("k", d), km.at[src], me.dev(z=src))
    ts[mine] = jnp.zeros(ts.shape[1:], F32)

    def finish(d):
        zz = (z + d) % 4
        for n in range(wide // 256):
            at = slice(n * 256, (n + 1) * 256)
            kept = c[zz, :, at] * km[zz, 0:1, at]
            ts[mine, :, at] += jnp.sum(kept * kept, axis=0, keepdims=True)
            top = jnp.max(kept, axis=0, keepdims=True)
            up = jnp.where(top > 0, 32767.0 / jnp.where(top > 0, top, 1.0), 0.0)
            cq[d, :, at] = jnp.round(kept * up).astype(jnp.int32).astype(jnp.int16)
            gsend[d, :, at] = top * (1.0 / 32767.0)
        if d:
            net.send(("c", d), cq.at[d], chunk(q_out, z), me.dev(z=zz))

    finish(1)
    finish(3)
    mate1(3)
    for piece in range(4):
        units(1 - yh, piece, (2,))
    finish(2)
    units(1 - yh, 3, (0,))
    finish(0)
    own = pltpu.make_async_copy(cq.at[0], chunk(q_out, z), local_sem)
    own.start()
    for d, dy in around:
        net.send(("t", d, dy), ts.at[mine], ts.at[mine], me.dev(x=(x + d) % 4, yl=(yl + dy) % 2))
    for d, dy in around:
        xx, yy = (x - d + 4) % 4, (yl + dy) % 2
        net.wait(("t", d, dy), ts.at[yy * 4 + xx], me.dev(x=xx, yl=yy))
    total = ((ts[0] + ts[1]) + (ts[2] + ts[3])) + ((ts[4] + ts[5]) + (ts[6] + ts[7]))
    scale = (rows * 32) / total
    for d in range(4):
        gsend[d, :, wide:] = scale
    gs[z] = gsend[0]
    for d in (1, 3, 2):
        net.send(("s", d), gsend.at[d], gs.at[z], me.dev(z=(z + d) % 4))
    own.wait()
    for d in (1, 3, 2):
        src = (z - d + 4) % 4
        net.wait(("s", d), gs.at[src], me.dev(z=src))
    gs_out[...] = gs[...]
    for d in (1, 3, 2):
        src = (z - d + 4) % 4
        net.wait(("c", d), chunk(q_out, src), me.dev(z=src))
    net.drain()


def body(flow, pattern, keep):
    rows, cols = flow.shape
    tile = cols // pattern.shape[1]
    wide = cols // 4
    vmem = pl.BlockSpec(memory_space=pltpu.VMEM)
    smem = pl.BlockSpec(memory_space=pltpu.SMEM)
    messages = 104
    coded, factors = pl.pallas_call(
        lambda *refs: kernel(tile, *refs),
        out_shape=(jax.ShapeDtypeStruct((rows, cols), jnp.int16), jax.ShapeDtypeStruct((4, 1, 2 * wide), F32)),
        in_specs=[vmem, smem, smem],
        out_specs=(pl.BlockSpec(memory_space=pl.ANY), vmem),
        scratch_shapes=[
            pltpu.VMEM((4, 4 * rows, cols), BF16),
            pltpu.VMEM((32 * rows, wide), BF16),
            pltpu.VMEM((rows, cols), BF16),
            pltpu.VMEM((3, rows, cols), BF16),
            pltpu.VMEM((3, rows, wide), BF16),
            pltpu.VMEM((3, rows, wide), BF16),
            pltpu.VMEM((4, rows, wide), F32),
            pltpu.VMEM((4, rows, wide), jnp.int16),
            pltpu.VMEM((4, 1, cols), F32),
            pltpu.VMEM((8, 1, cols), F32),
            pltpu.VMEM((1, cols), F32),
            pltpu.VMEM((8, cols), F32),
            pltpu.VMEM((4, 8, wide), F32),
            pltpu.VMEM((8, 1, wide), F32),
            pltpu.VMEM((4, 1, 2 * wide), F32),
            pltpu.VMEM((4, 1, 2 * wide), F32),
            pltpu.SemaphoreType.DMA((messages,)),
            pltpu.SemaphoreType.DMA((messages,)),
            pltpu.SemaphoreType.DMA,
        ],
        compiler_params=pltpu.CompilerParams(
            collective_id=0, has_side_effects=True, vmem_limit_bytes=50 * 1024 * 1024),
        name="cluster",
    )(flow, pattern, keep)
    down = factors[:, 0, :wide].reshape(1, cols)
    scale = factors[:, 0, wide:].reshape(1, cols)
    expanded = coded.astype(F32) * down
    return expanded * expanded * scale


def solution(mesh):
    return jax.shard_map(
        body,
        mesh=mesh,
        in_specs=(P("row", "col"), P("row", "col"), P("row", "col")),
        out_specs=P("row", "col"),
        check_vma=False,
    )
```

```python
import jax
import jax.numpy as jnp
from jax import lax
from jax.experimental import pallas as pl
from jax.experimental.pallas import tpu as pltpu
from jax.sharding import PartitionSpec as P

MESH = pl.DeviceIdType.MESH
F32 = jnp.float32
BF16 = jnp.bfloat16
RING = 6
ORDER = (
    "start", "mx", ("f", 0), "inv", ("home", 1), ("home", 2), "own", "nb0", "lx0", ("home", 3), ("f", 1), ("home", 4),
    ("f", 2), "z0a", ("f", 3), ("y", 0), ("y", 1), ("y", 2), ("fin", 0), ("f", 4), ("fin", 1), ("home", 5),
    ("home", 6), ("Lz", 0), ("fin", 2), ("home", 7), ("f", 5), ("E", 0), "z1a", ("r", 0), ("f", 6), ("r", 1),
    ("f", 7), "z1b", ("E", 1), ("Lz", 1), ("Lm", 0), ("r", 2), ("Lm", 1), ("E", 2), ("Lz", 2), ("Lm", 2), "z1c",
    ("E", 3), ("Lz", 3), ("Lm", 3), ("C", 1), ("C", 3), ("L2", 0), ("L2", 1), ("L2", 2), ("L2", 3), ("C", 2),
    ("C", 0), "tot",
)


class Place:
    def __init__(self):
        row, col = lax.axis_index("row"), lax.axis_index("col")
        self.row, self.col = row, col
        self.yl, self.z, self.x = row // 16, (row // 4) % 4, row % 4
        self.yh, self.c = col // 2, col % 2

    def dev(self, x=None, z=None, yl=None, yh=None, c=None):
        x = self.x if x is None else x
        z = self.z if z is None else z
        yl = self.yl if yl is None else yl
        yh = self.yh if yh is None else yh
        c = self.c if c is None else c
        return (yl * 16 + z * 4 + x, yh * 2 + c)


class Copies:
    def __init__(self, send_sem, recv_sem, me):
        self.send_sem, self.recv_sem, self.me = send_sem, recv_sem, me
        self.ids, self.sent, self.met = {}, [], set()

    def slot(self, name):
        return self.ids.setdefault(name, len(self.ids))

    def make(self, name, src, dst, dev):
        k = self.slot(name)
        return pltpu.make_async_remote_copy(
            src_ref=src, dst_ref=dst, send_sem=self.send_sem.at[k], recv_sem=self.recv_sem.at[k],
            device_id=dev, device_id_type=MESH)

    def send(self, name, src, dst, dev):
        copy = self.make(name, src, dst, dev)
        copy.start()
        self.sent.append(copy)

    def wait(self, name, landed, dev):
        self.make(name, landed, landed, dev).wait_recv()

    def need(self, name, landed, dev):
        if name not in self.met:
            self.met.add(name)
            self.wait(name, landed, dev)

    def drain(self):
        for copy in self.sent:
            copy.wait_send()


def kernel(tile, flow_hbm, pattern_hbm, keep_hbm, q_out, gs_out, flow, pattern, keep, a, b, m, araw, yraw, braw, xraw, craw, c, cq,
           xs, zs, inv, kx, km, ts, gsend, gs, send_sem, recv_sem, local_sem):
    me = Place()
    rows, cols = flow.shape
    nt = cols // tile
    half = rows // 2
    wide = cols // 4
    ring = RING * rows // 8
    parts = ((0, ring // 2), (ring // 2, ring // 2), (ring, rows - ring))
    x, z, yl, yh, core = me.x, me.z, me.yl, me.yh, me.c
    net = Copies(send_sem, recv_sem, me)
    zp, zm, z2 = (z + 1) % 4, (z + 3) % 4, (z + 2) % 4
    xp, xm, x2 = (x + 1) % 4, (x + 3) % 4, (x + 2) % 4
    around = [(d, dy) for dy in (0, 1) for d in range(4) if (d, dy) != (0, 0)]
    mate, across, beside = me.dev(c=1 - core), me.dev(yh=1 - yh), me.dev(yl=1 - yl)
    fetch = [pltpu.make_async_copy(src, dst, local_sem.at[k])
             for k, (src, dst) in enumerate(((flow_hbm, flow), (pattern_hbm, pattern), (keep_hbm, keep)))]
    for copy in fetch:
        copy.start()
    barrier = pltpu.get_barrier_semaphore()
    peers = ([me.dev(x=(x + d) % 4, yl=(yl + dy) % 2) for d, dy in around]
             + [me.dev(z=(z + d) % 4, yl=(yl + dy) % 2) for d, dy in around if d] + [mate, across])
    for dev in peers:
        pl.semaphore_signal(barrier, inc=1, device_id=dev, device_id_type=MESH)

    q0, q1 = yh * 2 + core, (1 - yh) * 2 + core
    z_mates = (z, zm, zp, z2)
    z_order = (z, zp, zm, z2)
    pieces = [(yl, zz) for zz in z_order] + [(1 - yl, zz) for zz in z_order]

    def block(yy, zz, xx):
        return yy * 16 + zz * 4 + xx

    def a_at(q, zz, start=0, size=rows):
        return a.at[q, pl.ds(pl.multiple_of(zz * rows + start, 16), size)]

    def b_at(yy, zz, xx, start=0, size=rows):
        return b.at[pl.ds(pl.multiple_of(block(yy, zz, xx) * rows + start, half), size)]

    def chunk(ref, j):
        return ref.at[:, pl.ds(pl.multiple_of(j * wide, wide), wide)]

    def eye(count, first_row, first_col):
        r = lax.broadcasted_iota(jnp.int32, (count, tile), 0)
        k = lax.broadcasted_iota(jnp.int32, (count, tile), 1)
        return (r - k == first_col - first_row).astype(F32)

    def normalise(dst, src, masses, count, first_row, col, first_tile):
        height = src.shape[0]

        def step(t, _):
            at = pl.ds(pl.multiple_of(t * tile, tile), tile)
            there = pl.ds(pl.multiple_of((first_tile + t) * tile, tile), tile)
            value = src[:, at].astype(F32) + eye(height, first_row, col * cols + (first_tile + t) * tile)
            dst[:, at] = (value * inv[masses, :, there]).astype(BF16)
            return _

        lax.fori_loop(0, count, step, 0)

    def normalise_b(yy, zz, xx, src):
        normalise(b_at(yy, zz, xx), src, 0, wide // tile, block(yy, zz, xx) * rows, me.col, z * (wide // tile))

    def normalise_a(zz, src):
        normalise(a_at(q0, zz), src, 0, nt, block(yl, zz, x) * rows, me.col, 0)

    def landed_x(i, k, start=0, size=rows):
        if i == 0:
            return xraw.at[k, pl.ds(start, size)]
        yy, zz = pieces[i]
        return b_at(yy, zz, (xm, xp, x2)[k], start, size)

    def sent_x(i, k, start=0, size=rows):
        if i == 0:
            return xraw.at[k, pl.ds(start, size)]
        yy, zz = pieces[i]
        return b_at(yy, zz, x if k < 2 else (xm if start == 0 else xp), start, size)

    def spread_x(i, src):
        net.send(("bx+", i), src, sent_x(i, 0), me.dev(x=xp))
        net.send(("bx-", i), src, sent_x(i, 1), me.dev(x=xm))

    def forward_x(i):
        net.wait(("bx+", i), landed_x(i, 0), me.dev(x=xm))
        net.send(("bf+", i), landed_x(i, 0, 0, half), sent_x(i, 2, 0, half), me.dev(x=xp))
        net.wait(("bx-", i), landed_x(i, 1), me.dev(x=xp))
        net.send(("bf-", i), landed_x(i, 1, half, half), sent_x(i, 2, half, half), me.dev(x=xm))

    def last_x(i):
        net.need(("bf+", i), landed_x(i, 2, 0, half), me.dev(x=xm))
        net.need(("bf-", i), landed_x(i, 2, half, half), me.dev(x=xp))

    def start():
        for copy in fetch:
            copy.wait()
        for t in range(nt):
            at = slice(t * tile, (t + 1) * tile)
            on = (pattern[0, t] > 0).astype(F32)
            masked = flow[:, at].astype(F32) * on
            m[:, at] = masked.astype(BF16)
            masked = masked + eye(rows, me.row * rows, me.col * cols + t * tile)
            xs[x, :, at] = jnp.sum(masked, axis=0, keepdims=True)
            kept = jnp.logical_or(keep[0, t] > 0, me.row == me.col * nt + t).astype(F32)
            kx[:, at] = jnp.broadcast_to(kept, (8, tile))
        km[z] = kx[:, pl.ds(pl.multiple_of(z * wide, wide), wide)]
        ts[yl * 4 + x] = jnp.zeros(ts.shape[1:], F32)
        pl.semaphore_wait(barrier, len(peers))
        for d in (1, 3, 2):
            net.send(("mx", d), xs.at[x], xs.at[x], me.dev(x=(x + d) % 4))
        net.send("bz+", chunk(m, zp), braw.at[0], me.dev(z=zp))
        net.send("bz-", chunk(m, zm), braw.at[1], me.dev(z=zm))
        spread_x(0, chunk(m, z))

    def masses_x():
        for d in (1, 3, 2):
            src = (x - d + 4) % 4
            net.wait(("mx", d), xs.at[src], me.dev(x=src))
        here = yl * 4 + z
        zs[here] = (xs[0] + xs[1]) + (xs[2] + xs[3])
        for d, dy in around:
            net.send(("mz", d, dy), zs.at[here], zs.at[here], me.dev(z=(z + d) % 4, yl=(yl + dy) % 2))
        for p, (first, size) in enumerate(parts):
            at = pl.ds(first, size)
            net.send(("ay", p), m.at[at], yraw.at[at], across)
            if p == 0:
                net.send(("by", 0), chunk(m, z), craw, beside)
        net.send("bz2", chunk(m, z2), braw.at[2], me.dev(z=z2))
        for d in (1, 3, 2):
            net.send(("k", d), chunk(kx, (z + d) % 4), km.at[z], me.dev(z=(z + d) % 4))
        for first in (0, 1):
            for name, h, k, to in (("az0+", first, 0, zp), ("az0-", 1 - first, 1, zm)):
                at = pl.ds(h * half, half)
                net.send((name, h), m.at[at], araw.at[k, at], me.dev(z=to))

    def masses_z():
        for d, dy in around:
            zz, yy = (z - d + 4) % 4, (yl + dy) % 2
            net.wait(("mz", d, dy), zs.at[yy * 4 + zz], me.dev(z=zz, yl=yy))
        mass = ((zs[0] + zs[1]) + (zs[2] + zs[3])) + ((zs[4] + zs[5]) + (zs[6] + zs[7]))
        inv[0] = 1.0 / mass
        net.send("iv", inv.at[0], inv.at[1], across)

    def home(i):
        yy, zz = pieces[i]
        piece = b_at(yy, zz, x)
        if i in (1, 2, 3):
            name, k, src = {1: ("bz-", 1, zp), 2: ("bz+", 0, zm), 3: ("bz2", 2, z2)}[i]
            net.wait(name, braw.at[k], me.dev(z=src))
            normalise_b(yy, zz, x, braw.at[k])
            spread_x(i, piece)
            net.send(("by", i), piece, piece, beside)
        else:
            net.wait(("by", i - 4), craw if i == 4 else piece, beside)
            if i == 4:
                normalise_b(yy, zz, x, craw)
            spread_x(i, piece)

    def own_a():
        normalise_a(z, m)
        net.send(("ac0", 0), a_at(q0, z), a_at(q0, z), mate)

    def own_b():
        normalise_b(yl, z, x, chunk(m, z))
        c[...] = jnp.zeros(c.shape, F32)

    def raw_x():
        last_x(0)
        for k, xx in enumerate((xm, xp, x2)):
            normalise_b(yl, z, xx, xraw.at[k])

    def take_z0(k, h):
        at = pl.ds(h * half, half)
        if k == 0:
            net.need(("az0+", h), araw.at[0, at], me.dev(z=zm))
            if h == 0:
                net.send("af0+", araw.at[0, at], araw.at[2, at], me.dev(z=zp))
        elif k == 1:
            net.need(("az0-", h), araw.at[1, at], me.dev(z=zp))
            if h == 1:
                net.send("af0-", araw.at[1, at], araw.at[2, at], me.dev(z=zm))
        elif h == 0:
            net.need("af0+", araw.at[2, at], me.dev(z=zm))
        else:
            net.need("af0-", araw.at[2, at], me.dev(z=zp))

    def first_z0():
        take_z0(0, 0)
        take_z0(1, 1)

    def finish_z0(k):
        if k == 2:
            take_z0(2, 0)
            take_z0(2, 1)
        else:
            take_z0(k, 1 - k)
        zz = (zm, zp, z2)[k]
        normalise_a(zz, araw.at[k])
        start, size = parts[2]
        net.send(("ar", k), a_at(q0, zz, start, size), a_at(q0, zz, start, size), across)
        net.send(("ac0", k + 1), a_at(q0, zz), a_at(q0, zz), mate)

    def to_mate(k, p):
        zz = z_mates[k]
        net.send(("ac1", k, p), a_at(q1, zz, *parts[p]), a_at(q1, zz, *parts[p]), mate)

    def take_y(p):
        at = a_at(q1, z, *parts[p])
        first, size = parts[p]
        raw = yraw.at[pl.ds(first, size)]
        net.wait(("ay", p), raw, across)
        net.need("iv", inv.at[1], across)
        normalise(at, raw, 1, nt, block(yl, z, x) * rows + first, q1, 0)
        if p < 2:
            net.send(("az1+", p), at, at, me.dev(z=zp))
            net.send(("az1-", p), at, at, me.dev(z=zm))
        to_mate(0, p)

    def take_rest(k):
        net.wait(("ar", k), a_at(q1, (zm, zp, z2)[k], *parts[2]), across)
        to_mate(k + 1, 2)

    def take_z1(k, p):
        at = a_at(q1, (zm, zp, z2)[k], *parts[p])
        if k == 0:
            net.wait(("az1+", p), at, me.dev(z=zm))
            if p == 0:
                net.send("af1+", at, at, me.dev(z=zp))
        elif k == 1:
            net.wait(("az1-", p), at, me.dev(z=zp))
            if p == 1:
                net.send("af1-", at, at, me.dev(z=zm))
        elif p == 0:
            net.wait("af1+", at, me.dev(z=zm))
        else:
            net.wait("af1-", at, me.dev(z=zp))
        to_mate(k + 1, p)

    def first_z1():
        take_z1(0, 0)
        take_z1(1, 1)

    def ready_b(j):
        last_x(j)
        last_x(j + 4)

    def mate0():
        for k in range(4):
            net.need(("ac0", k), a_at(yh * 2 + 1 - core, z_mates[k]), mate)

    def mate1(k):
        for p in (0, 1, 2):
            net.need(("ac1", k, p), a_at((1 - yh) * 2 + 1 - core, z_mates[k], *parts[p]), mate)

    def units(yy, piece, ks):
        zi = z_order[piece]
        deep = 4 * rows
        left_at = pl.ds(pl.multiple_of((zi % 2) * deep, deep), deep)
        right_at = pl.ds(pl.multiple_of((yy * 4 + zi) * deep, deep), deep)
        q = yy * 2 + zi // 2

        def step(j, _):
            k, n = j // 2, j % 2
            zz = (z + (ks[0] if len(ks) == 1 else k if len(ks) == 4 else ks[0] + 2 * k)) % 4
            at = pl.ds(pl.multiple_of(n * 256, 256), 256)
            left = a[q, pl.ds(pl.multiple_of(zz * rows, rows), rows), left_at]
            value = jnp.dot(left, b[right_at, at], preferred_element_type=F32)
            c[zz, :, at] += value
            return _

        lax.fori_loop(0, 2 * len(ks), step, 0)

    def early(j):
        mate0()
        ready_b(j)
        units(yh, j, (0, 1, 2, 3))

    def late(j, ks):
        for k in ks:
            mate1({0: 0, 3: 1, 1: 2, 2: 3}[k])
        ready_b(j)
        units(1 - yh, j, ks)

    mine = yl * 4 + x

    def finish(d):
        zz = (z + d) % 4
        if d:
            net.need(("k", (4 - d) % 4), km.at[zz], me.dev(z=zz))
        for n in range(wide // 256):
            at = slice(n * 256, (n + 1) * 256)
            kept = c[zz, :, at] * km[zz, 0:1, at]
            ts[mine, :, at] += jnp.sum(kept * kept, axis=0, keepdims=True)
            top = jnp.max(kept, axis=0, keepdims=True)
            up = jnp.where(top > 0, 32767.0 / jnp.where(top > 0, top, 1.0), 0.0)
            cq[d, :, at] = jnp.round(kept * up).astype(jnp.int32).astype(jnp.int16)
            gsend[d, :, at] = top * (1.0 / 32767.0)
        if d:
            net.send(("c", d), cq.at[d], chunk(q_out, z), me.dev(z=zz))

    def total():
        own = pltpu.make_async_copy(cq.at[0], chunk(q_out, z), local_sem.at[0])
        own.start()
        for d, dy in around:
            net.send(("t", d, dy), ts.at[mine], ts.at[mine], me.dev(x=(x + d) % 4, yl=(yl + dy) % 2))
        for d, dy in around:
            xx, yy = (x - d + 4) % 4, (yl + dy) % 2
            net.wait(("t", d, dy), ts.at[yy * 4 + xx], me.dev(x=xx, yl=yy))
        whole = ((ts[0] + ts[1]) + (ts[2] + ts[3])) + ((ts[4] + ts[5]) + (ts[6] + ts[7]))
        scale = (rows * 32) / whole
        for d in range(4):
            gsend[d, :, wide:] = scale
        gs[z] = gsend[0]
        for d in (1, 3, 2):
            net.send(("s", d), gsend.at[d], gs.at[z], me.dev(z=(z + d) % 4))
        own.wait()
        for d in (1, 3, 2):
            src = (z - d + 4) % 4
            net.wait(("s", d), gs.at[src], me.dev(z=src))
        gs_out[...] = gs[...]
        for d in (1, 3, 2):
            src = (z - d + 4) % 4
            net.wait(("c", d), chunk(q_out, src), me.dev(z=src))
        net.drain()

    def later_z1():
        take_z1(0, 1)
        take_z1(1, 0)

    steps = {"start": start, "mx": masses_x, "inv": masses_z, "own": own_a, "nb0": own_b, "lx0": raw_x, "z0a": first_z0,
             "z1a": first_z1, "tot": total}
    for step in ORDER:
        if step in steps:
            steps[step]()
        elif step == "z1b":
            later_z1()
        elif step == "z1c":
            take_z1(2, 0)
            take_z1(2, 1)
        else:
            {"home": home, "f": forward_x, "y": take_y, "fin": finish_z0, "r": take_rest, "E": early, "C": finish,
             "Lz": lambda j: late(j, (0,)), "Lm": lambda j: late(j, (1, 3)), "L2": lambda j: late(j, (2,))}[step[0]](step[1])

def body(flow, pattern, keep):
    rows, cols = flow.shape
    tile = cols // pattern.shape[1]
    wide = cols // 4
    vmem = pl.BlockSpec(memory_space=pltpu.VMEM)
    anyspace = pl.BlockSpec(memory_space=pl.ANY)
    messages = 104
    coded, factors = pl.pallas_call(
        lambda *refs: kernel(tile, *refs),
        out_shape=(jax.ShapeDtypeStruct((rows, cols), jnp.int16), jax.ShapeDtypeStruct((4, 1, 2 * wide), F32)),
        in_specs=[pl.BlockSpec(memory_space=pltpu.HBM)] * 3,
        out_specs=(anyspace, vmem),
        scratch_shapes=[
            pltpu.VMEM((rows, cols), BF16),
            pltpu.SMEM(pattern.shape, jnp.int32),
            pltpu.SMEM(keep.shape, jnp.int32),
            pltpu.VMEM((4, 4 * rows, cols), BF16),
            pltpu.VMEM((32 * rows, wide), BF16),
            pltpu.VMEM((rows, cols), BF16),
            pltpu.VMEM((3, rows, cols), BF16),
            pltpu.VMEM((rows, cols), BF16),
            pltpu.VMEM((3, rows, wide), BF16),
            pltpu.VMEM((3, rows, wide), BF16),
            pltpu.VMEM((rows, wide), BF16),
            pltpu.VMEM((4, rows, wide), F32),
            pltpu.VMEM((4, rows, wide), jnp.int16),
            pltpu.VMEM((4, 1, cols), F32),
            pltpu.VMEM((8, 1, cols), F32),
            pltpu.VMEM((2, 1, cols), F32),
            pltpu.VMEM((8, cols), F32),
            pltpu.VMEM((4, 8, wide), F32),
            pltpu.VMEM((8, 1, wide), F32),
            pltpu.VMEM((4, 1, 2 * wide), F32),
            pltpu.VMEM((4, 1, 2 * wide), F32),
            pltpu.SemaphoreType.DMA((messages,)),
            pltpu.SemaphoreType.DMA((messages,)),
            pltpu.SemaphoreType.DMA((3,)),
        ],
        compiler_params=pltpu.CompilerParams(
            collective_id=0, has_side_effects=True, vmem_limit_bytes=52000 * 1024),
        name="cluster",
    )(*(pltpu.with_memory_space_constraint(v, pltpu.HBM) for v in (flow, pattern, keep)))
    down = factors[:, 0, :wide].reshape(1, cols)
    scale = factors[:, 0, wide:].reshape(1, cols)
    expanded = coded.astype(F32) * down
    return expanded * expanded * scale


def solution(mesh):
    return jax.shard_map(
        body,
        mesh=mesh,
        in_specs=(P("row", "col"), P("row", "col"), P("row", "col")),
        out_specs=P("row", "col"),
        check_vma=False,
    )
```

```python
import jax
import jax.numpy as jnp
from jax import lax
from jax.experimental import pallas as pl
from jax.experimental.pallas import tpu as pltpu
from jax.sharding import PartitionSpec as P

MESH = pl.DeviceIdType.MESH
F32 = jnp.float32
BF16 = jnp.bfloat16
RING = 7
ORDER = (
    "start", "mx", ("f", 0), "inv", ("home", 1), ("home", 2), "own", "nb0", "lx0", "z0f", ("f", 1), "z0a",
    ("home", 4), ("home", 3), ("f", 2), "z0b", ("fin", 0), ("fin", 1), ("f", 4), ("y", 0), ("y", 1), ("y", 2),
    ("fin", 2), ("f", 3), ("home", 5), ("home", 6), ("E", 0), "z1a", ("home", 7), ("f", 5), ("r", 0), "z1b", ("r", 1),
    ("f", 6), ("r", 2), ("L", 0), ("f", 7), ("E", 1), "z1c", ("L", 1), ("E", 2), ("L", 2), ("E", 3), ("O", 0),
    ("O", 1), ("O", 2), ("L", 3), ("O", 3), ("C", 1), ("C", 3), ("C", 2), ("C", 0), "tot",
)


class Place:
    def __init__(self):
        row, col = lax.axis_index("row"), lax.axis_index("col")
        self.row, self.col = row, col
        self.yl, self.z, self.x = row // 16, (row // 4) % 4, row % 4
        self.yh, self.c = col // 2, col % 2

    def dev(self, x=None, z=None, yl=None, yh=None, c=None):
        x = self.x if x is None else x
        z = self.z if z is None else z
        yl = self.yl if yl is None else yl
        yh = self.yh if yh is None else yh
        c = self.c if c is None else c
        return (yl * 16 + z * 4 + x, yh * 2 + c)


class Copies:
    def __init__(self, send_sem, recv_sem, me):
        self.send_sem, self.recv_sem, self.me = send_sem, recv_sem, me
        self.ids, self.sent, self.met = {}, [], set()

    def slot(self, name):
        return self.ids.setdefault(name, len(self.ids))

    def make(self, name, src, dst, dev):
        k = self.slot(name)
        return pltpu.make_async_remote_copy(
            src_ref=src, dst_ref=dst, send_sem=self.send_sem.at[k], recv_sem=self.recv_sem.at[k],
            device_id=dev, device_id_type=MESH)

    def send(self, name, src, dst, dev):
        copy = self.make(name, src, dst, dev)
        copy.start()
        self.sent.append(copy)

    def wait(self, name, landed, dev):
        self.make(name, landed, landed, dev).wait_recv()

    def need(self, name, landed, dev):
        if name not in self.met:
            self.met.add(name)
            self.wait(name, landed, dev)

    def drain(self):
        for copy in self.sent:
            copy.wait_send()


def kernel(tile, flow_hbm, pattern_hbm, keep_hbm, q_out, gs_out, flow, pattern, keep, a, b, m, araw, yraw, xraw, craw, c, cq,
           xs, zs, inv, kx, km, ts, gsend, gs, send_sem, recv_sem, local_sem):
    me = Place()
    rows, cols = flow.shape
    nt = cols // tile
    half = rows // 2
    wide = cols // 4
    ring = RING * rows // 8
    parts = ((0, ring // 2), (ring // 2, ring // 2), (ring, rows - ring))
    x, z, yl, yh, core = me.x, me.z, me.yl, me.yh, me.c
    net = Copies(send_sem, recv_sem, me)
    zp, zm, z2 = (z + 1) % 4, (z + 3) % 4, (z + 2) % 4
    xp, xm, x2 = (x + 1) % 4, (x + 3) % 4, (x + 2) % 4
    around = [(d, dy) for dy in (0, 1) for d in range(4) if (d, dy) != (0, 0)]
    mate, across, beside = me.dev(c=1 - core), me.dev(yh=1 - yh), me.dev(yl=1 - yl)
    fetch = [pltpu.make_async_copy(src, dst, local_sem.at[k])
             for k, (src, dst) in enumerate(((flow_hbm, flow), (pattern_hbm, pattern), (keep_hbm, keep)))]
    for copy in fetch:
        copy.start()
    barrier = pltpu.get_barrier_semaphore()
    peers = ([me.dev(x=(x + d) % 4, yl=(yl + dy) % 2) for d, dy in around]
             + [me.dev(z=(z + d) % 4, yl=(yl + dy) % 2) for d, dy in around if d] + [mate, across])
    for dev in peers:
        pl.semaphore_signal(barrier, inc=1, device_id=dev, device_id_type=MESH)

    q0, q1 = yh * 2 + core, (1 - yh) * 2 + core
    z_mates = (z, zm, zp, z2)
    z_order = (z, zp, zm, z2)
    pieces = [(yl, zz) for zz in z_order] + [(1 - yl, zz) for zz in z_order]

    def block(yy, zz, xx):
        return yy * 16 + zz * 4 + xx

    def a_at(q, k, start=0, size=rows):
        return a.at[q, pl.ds(k * rows + start, size)]

    def b_at(yy, zz, xx, start=0, size=rows):
        return b.at[pl.ds(pl.multiple_of(block(yy, zz, xx) * rows + start, half), size)]

    def chunk(ref, j):
        return ref.at[:, pl.ds(pl.multiple_of(j * wide, wide), wide)]

    def eye(count, first_row, first_col):
        r = lax.broadcasted_iota(jnp.int32, (count, tile), 0)
        k = lax.broadcasted_iota(jnp.int32, (count, tile), 1)
        return (r - k == first_col - first_row).astype(F32)

    def normalise(dst, src, masses, count, first_row, col, first_tile):
        height = src.shape[0]

        def step(t, _):
            at = pl.ds(pl.multiple_of(t * tile, tile), tile)
            there = pl.ds(pl.multiple_of((first_tile + t) * tile, tile), tile)
            value = src[:, at].astype(F32) + eye(height, first_row, col * cols + (first_tile + t) * tile)
            dst[:, at] = (value * inv[masses, :, there]).astype(BF16)
            return _

        lax.fori_loop(0, count, step, 0)

    def normalise_b(yy, zz, xx, src):
        normalise(b_at(yy, zz, xx), src, 0, wide // tile, block(yy, zz, xx) * rows, me.col, z * (wide // tile))

    def normalise_a(k, src):
        normalise(a_at(q0, k), src, 0, nt, block(yl, z_mates[k], x) * rows, me.col, 0)

    def landed_x(i, k, start=0, size=rows):
        if i == 0:
            return xraw.at[k, pl.ds(start, size)]
        yy, zz = pieces[i]
        return b_at(yy, zz, (xm, xp, x2)[k], start, size)

    def sent_x(i, k, start=0, size=rows):
        if i == 0:
            return xraw.at[k, pl.ds(start, size)]
        yy, zz = pieces[i]
        return b_at(yy, zz, x if k < 2 else (xm if start == 0 else xp), start, size)

    def spread_x(i, src):
        net.send(("bx+", i), src, sent_x(i, 0), me.dev(x=xp))
        net.send(("bx-", i), src, sent_x(i, 1), me.dev(x=xm))

    def forward_x(i):
        net.wait(("bx+", i), landed_x(i, 0), me.dev(x=xm))
        net.send(("bf+", i), landed_x(i, 0, 0, half), sent_x(i, 2, 0, half), me.dev(x=xp))
        net.wait(("bx-", i), landed_x(i, 1), me.dev(x=xp))
        net.send(("bf-", i), landed_x(i, 1, half, half), sent_x(i, 2, half, half), me.dev(x=xm))

    def last_x(i):
        net.need(("bf+", i), landed_x(i, 2, 0, half), me.dev(x=xm))
        net.need(("bf-", i), landed_x(i, 2, half, half), me.dev(x=xp))

    def start():
        for copy in fetch:
            copy.wait()
        for t in range(nt):
            at = slice(t * tile, (t + 1) * tile)
            on = (pattern[0, t] > 0).astype(F32)
            masked = flow[:, at].astype(F32) * on
            m[:, at] = masked.astype(BF16)
            diagonal = me.row == me.col * nt + t
            xs[x, :, at] = jnp.sum(masked, axis=0, keepdims=True) + diagonal.astype(F32)
            kept = jnp.logical_or(keep[0, t] > 0, diagonal).astype(F32)
            kx[:, at] = jnp.broadcast_to(kept, (8, tile))
        km[z] = kx[:, pl.ds(pl.multiple_of(z * wide, wide), wide)]
        ts[yl * 4 + x] = jnp.zeros(ts.shape[1:], F32)
        pl.semaphore_wait(barrier, len(peers))
        for d in (1, 3, 2):
            net.send(("mx", d), xs.at[x], xs.at[x], me.dev(x=(x + d) % 4))
        send_z0(0)
        spread_x(0, chunk(m, z))

    def masses_x():
        for d in (1, 3, 2):
            src = (x - d + 4) % 4
            net.wait(("mx", d), xs.at[src], me.dev(x=src))
        here = yl * 4 + z
        zs[here] = (xs[0] + xs[1]) + (xs[2] + xs[3])
        for d, dy in around:
            net.send(("mz", d, dy), zs.at[here], zs.at[here], me.dev(z=(z + d) % 4, yl=(yl + dy) % 2))
        for p, (first, size) in enumerate(parts):
            at = pl.ds(first, size)
            net.send(("ay", p), m.at[at], yraw.at[at], across)
            if p == 0:
                net.send(("by", 0), chunk(m, z), craw, beside)
        for d in (1, 3, 2):
            net.send(("k", d), chunk(kx, (z + d) % 4), km.at[z], me.dev(z=(z + d) % 4))
        send_z0(1)
        send_z0(2)

    def masses_z():
        for d, dy in around:
            zz, yy = (z - d + 4) % 4, (yl + dy) % 2
            net.wait(("mz", d, dy), zs.at[yy * 4 + zz], me.dev(z=zz, yl=yy))
        mass = ((zs[0] + zs[1]) + (zs[2] + zs[3])) + ((zs[4] + zs[5]) + (zs[6] + zs[7]))
        inv[0] = 1.0 / mass
        net.send("iv", inv.at[0], inv.at[1], across)

    def home(i):
        yy, zz = pieces[i]
        piece = b_at(yy, zz, x)
        if i in (1, 2, 3):
            k = {1: 1, 2: 0, 3: 2}[i]
            if k < 2:
                take_z0(k, 0)
            else:
                last_z0(0)
            normalise_b(yy, zz, x, chunk(araw.at[k], z))
            spread_x(i, piece)
            net.send(("by", i), piece, piece, beside)
        else:
            net.wait(("by", i - 4), craw if i == 4 else piece, beside)
            if i == 4:
                normalise_b(yy, zz, x, craw)
            spread_x(i, piece)

    def own_a():
        normalise_a(0, m)
        net.send(("ac0", 0), a_at(q0, 0), a_at(q0, 0), mate)

    def own_b():
        normalise_b(yl, z, x, chunk(m, z))
        c[...] = jnp.zeros(c.shape, F32)

    def raw_x():
        last_x(0)
        for k, xx in enumerate((xm, xp, x2)):
            normalise_b(yl, z, xx, xraw.at[k])

    plus, minus = (zp, z2, z, zm), (zm, z2, z, zp)

    def send_z0(n):
        net.send(("az0+", n), chunk(m, plus[n]), chunk(araw.at[0], plus[n]), me.dev(z=zp))
        net.send(("az0-", n), chunk(m, minus[n]), chunk(araw.at[1], minus[n]), me.dev(z=zm))

    def take_z0(k, n):
        if k == 0:
            net.need(("az0+", n), chunk(araw.at[0], (z, zp, zm, z2)[n]), me.dev(z=zm))
        else:
            net.need(("az0-", n), chunk(araw.at[1], (z, zm, zp, z2)[n]), me.dev(z=zp))

    def rows_of(ref, h):
        return ref.at[pl.ds(h * half, half)]

    def forward_z0(n):
        take_z0(0, n)
        j = (z, zp, zm, z2)[n]
        net.send(("af0+", n), rows_of(chunk(araw.at[0], j), 0), rows_of(chunk(araw.at[2], j), 0), me.dev(z=zp))
        take_z0(1, n)
        j = (z, zm, zp, z2)[n]
        net.send(("af0-", n), rows_of(chunk(araw.at[1], j), 1), rows_of(chunk(araw.at[2], j), 1), me.dev(z=zm))

    def last_z0(f):
        n = (1, 0, 2, 3)[f]
        net.need(("af0+", n), rows_of(chunk(araw.at[2], (zm, z, z2, zp)[n]), 0), me.dev(z=zm))
        net.need(("af0-", n), rows_of(chunk(araw.at[2], (zp, z, z2, zm)[n]), 1), me.dev(z=zp))

    def first_z0():
        forward_z0(1)
        send_z0(3)

    def middle_z0():
        forward_z0(0)
        forward_z0(2)

    def finish_z0(k):
        if k == 2:
            for f in range(4):
                last_z0(f)
        normalise_a(k + 1, araw.at[k])
        rest = a_at(q0, k + 1, *parts[2])
        net.send(("ar", k), rest, rest, across)
        net.send(("ac0", k + 1), a_at(q0, k + 1), a_at(q0, k + 1), mate)

    def to_mate(k, p):
        net.send(("ac1", k, p), a_at(q1, k, *parts[p]), a_at(q1, k, *parts[p]), mate)

    def take_y(p):
        at = a_at(q1, 0, *parts[p])
        first, size = parts[p]
        raw = yraw.at[pl.ds(first, size)]
        net.wait(("ay", p), raw, across)
        net.need("iv", inv.at[1], across)
        normalise(at, raw, 1, nt, block(yl, z, x) * rows + first, q1, 0)
        if p < 2:
            net.send(("az1+", p), at, a_at(q1, 1, *parts[p]), me.dev(z=zp))
            net.send(("az1-", p), at, a_at(q1, 2, *parts[p]), me.dev(z=zm))
        to_mate(0, p)

    def take_rest(k):
        net.wait(("ar", k), a_at(q1, k + 1, *parts[2]), across)
        to_mate(k + 1, 2)

    def take_z1(k, p):
        at = a_at(q1, k + 1, *parts[p])
        if k == 0:
            net.wait(("az1+", p), at, me.dev(z=zm))
            if p == 0:
                net.send("af1+", at, a_at(q1, 3, *parts[p]), me.dev(z=zp))
        elif k == 1:
            net.wait(("az1-", p), at, me.dev(z=zp))
            if p == 1:
                net.send("af1-", at, a_at(q1, 3, *parts[p]), me.dev(z=zm))
        elif p == 0:
            net.wait("af1+", at, me.dev(z=zm))
        else:
            net.wait("af1-", at, me.dev(z=zp))
        to_mate(k + 1, p)

    def first_z1():
        take_z1(0, 0)
        take_z1(1, 1)

    def ready_b(j):
        last_x(j)
        last_x(j + 4)

    def mate0():
        for k in range(4):
            net.need(("ac0", k), a_at(yh * 2 + 1 - core, k), mate)

    def mate1(k):
        for p in (0, 1, 2):
            net.need(("ac1", k, p), a_at((1 - yh) * 2 + 1 - core, k, *parts[p]), mate)

    def units(yy, piece, first, count):
        zi = z_order[piece]
        deep = 4 * rows
        left = a[yy * 2 + zi // 2, pl.ds(first * rows, count * rows), pl.ds(pl.multiple_of((zi % 2) * deep, deep), deep)]
        right = b[pl.ds(pl.multiple_of((yy * 4 + zi) * deep, deep), deep)]
        c[pl.ds(first * rows, count * rows)] += jnp.dot(left, right, preferred_element_type=F32)

    def early(j):
        mate0()
        ready_b(j)
        units(yh, j, 0, 4)

    def late(j, first, count):
        for k in range(first, first + count):
            mate1(k)
        ready_b(j)
        units(1 - yh, j, first, count)

    mine = yl * 4 + x

    def finish(d):
        zz = (z + d) % 4
        if d:
            net.need(("k", (4 - d) % 4), km.at[zz], me.dev(z=zz))
        slot = (0, 2, 3, 1)[d]
        kept = c[slot * rows:(slot + 1) * rows] * km[zz, 0:1]
        ts[mine] += jnp.sum(kept * kept, axis=0, keepdims=True)
        top = jnp.max(kept, axis=0, keepdims=True)
        up = jnp.where(top > 0, 32767.0 / jnp.where(top > 0, top, 1.0), 0.0)
        cq[d] = jnp.round(kept * up).astype(jnp.int32).astype(jnp.int16)
        gsend[d, :, :wide] = top * (1.0 / 32767.0)
        if d:
            net.send(("c", d), cq.at[d], chunk(q_out, z), me.dev(z=zz))

    def total():
        own = pltpu.make_async_copy(cq.at[0], chunk(q_out, z), local_sem.at[0])
        own.start()
        for d, dy in around:
            net.send(("t", d, dy), ts.at[mine], ts.at[mine], me.dev(x=(x + d) % 4, yl=(yl + dy) % 2))
        for d, dy in around:
            xx, yy = (x - d + 4) % 4, (yl + dy) % 2
            net.wait(("t", d, dy), ts.at[yy * 4 + xx], me.dev(x=xx, yl=yy))
        whole = ((ts[0] + ts[1]) + (ts[2] + ts[3])) + ((ts[4] + ts[5]) + (ts[6] + ts[7]))
        scale = (rows * 32) / whole
        for d in range(4):
            gsend[d, :, wide:] = scale
        gs[z] = gsend[0]
        for d in (1, 3, 2):
            net.send(("s", d), gsend.at[d], gs.at[z], me.dev(z=(z + d) % 4))
        own.wait()
        for d in (1, 3, 2):
            src = (z - d + 4) % 4
            net.wait(("s", d), gs.at[src], me.dev(z=src))
        gs_out[...] = gs[...]
        for d in (1, 3, 2):
            src = (z - d + 4) % 4
            net.wait(("c", d), chunk(q_out, src), me.dev(z=src))
        net.drain()

    def later_z1():
        take_z1(0, 1)
        take_z1(1, 0)

    steps = {"start": start, "mx": masses_x, "inv": masses_z, "own": own_a, "nb0": own_b, "lx0": raw_x, "z0f": first_z0,
             "z0a": middle_z0, "z0b": lambda: forward_z0(3), "z1a": first_z1, "tot": total}
    for step in ORDER:
        if step in steps:
            steps[step]()
        elif step == "z1b":
            later_z1()
        elif step == "z1c":
            take_z1(2, 0)
            take_z1(2, 1)
        else:
            {"home": home, "f": forward_x, "y": take_y, "fin": finish_z0, "r": take_rest, "E": early, "C": finish,
             "L": lambda j: late(j, 0, 3), "O": lambda j: late(j, 3, 1)}[step[0]](step[1])

def body(flow, pattern, keep):
    rows, cols = flow.shape
    tile = cols // pattern.shape[1]
    wide = cols // 4
    vmem = pl.BlockSpec(memory_space=pltpu.VMEM)
    anyspace = pl.BlockSpec(memory_space=pl.ANY)
    messages = 112
    coded, factors = pl.pallas_call(
        lambda *refs: kernel(tile, *refs),
        out_shape=(jax.ShapeDtypeStruct((rows, cols), jnp.int16), jax.ShapeDtypeStruct((4, 1, 2 * wide), F32)),
        in_specs=[pl.BlockSpec(memory_space=pltpu.HBM)] * 3,
        out_specs=(anyspace, vmem),
        scratch_shapes=[
            pltpu.VMEM((rows, cols), BF16),
            pltpu.SMEM(pattern.shape, jnp.int32),
            pltpu.SMEM(keep.shape, jnp.int32),
            pltpu.VMEM((4, 4 * rows, cols), BF16),
            pltpu.VMEM((32 * rows, wide), BF16),
            pltpu.VMEM((rows, cols), BF16),
            pltpu.VMEM((3, rows, cols), BF16),
            pltpu.VMEM((rows, cols), BF16),
            pltpu.VMEM((3, rows, wide), BF16),
            pltpu.VMEM((rows, wide), BF16),
            pltpu.VMEM((4 * rows, wide), F32),
            pltpu.VMEM((4, rows, wide), jnp.int16),
            pltpu.VMEM((4, 1, cols), F32),
            pltpu.VMEM((8, 1, cols), F32),
            pltpu.VMEM((2, 1, cols), F32),
            pltpu.VMEM((8, cols), F32),
            pltpu.VMEM((4, 8, wide), F32),
            pltpu.VMEM((8, 1, wide), F32),
            pltpu.VMEM((4, 1, 2 * wide), F32),
            pltpu.VMEM((4, 1, 2 * wide), F32),
            pltpu.SemaphoreType.DMA((messages,)),
            pltpu.SemaphoreType.DMA((messages,)),
            pltpu.SemaphoreType.DMA((3,)),
        ],
        compiler_params=pltpu.CompilerParams(
            collective_id=0, has_side_effects=True, vmem_limit_bytes=52000 * 1024),
        name="cluster",
    )(*(pltpu.with_memory_space_constraint(v, pltpu.HBM) for v in (flow, pattern, keep)))
    down = factors[:, 0, :wide].reshape(1, cols)
    scale = factors[:, 0, wide:].reshape(1, cols)
    expanded = coded.astype(F32) * down
    return expanded * expanded * scale


def solution(mesh):
    return jax.shard_map(
        body,
        mesh=mesh,
        in_specs=(P("row", "col"), P("row", "col"), P("row", "col")),
        out_specs=P("row", "col"),
        check_vma=False,
    )
```

```python
import jax
import jax.numpy as jnp
from jax import lax
from jax.experimental import pallas as pl
from jax.experimental.pallas import tpu as pltpu
from jax.sharding import PartitionSpec as P

MESH = pl.DeviceIdType.MESH
F32 = jnp.float32
BF16 = jnp.bfloat16
RING = 7
ORDER = (
    ("start",), ("mx",), ("sb", 0), ("sb", 1), ("sy", 1), ("f", 0, 0), ("f", 0, 1), ("inv",), ("home", 4, 0),
    ("home", 2, 1), ("g", 0), ("home", 1, 0), ("g", 1), ("own",), ("sa", 2), ("home", 4, 1), ("sa", 3),
    ("home", 3, 1), ("sy", 0), ("y", 1), ("f", 1, 0), ("g", 2), ("home", 3, 0), ("home", 5, 0), ("f", 4, 1),
    ("lx", 1), ("home", 2, 0), ("fin", 0), ("fin", 1), ("home", 7, 1), ("home", 1, 1), ("g", 3), ("lx", 0), ("sy", 2),
    ("f", 7, 1), ("f", 2, 0), ("f", 5, 0), ("y", 0), ("f", 1, 1), ("nb0",), ("z1", 1), ("f", 4, 0), ("f", 3, 1),
    ("home", 7, 0), ("fin", 2), ("f", 3, 0), ("r", 1), ("home", 6, 0), ("z1", 0), ("f", 7, 0), ("E", 1, 0),
    ("home", 6, 1), ("E", 0, 0), ("E", 0, 1), ("f", 6, 0), ("r", 0), ("y", 2), ("E", 3, 1), ("home", 5, 1), ("zo", 1),
    ("L", 1, 0), ("r", 2), ("L", 3, 0), ("f", 6, 1), ("E", 3, 0), ("L", 2, 0), ("L", 0, 0), ("f", 2, 1), ("zo", 0),
    ("E", 2, 0), ("C", 1, 0), ("C", 0, 0), ("f", 5, 1), ("L", 3, 1), ("L", 0, 1), ("O", 2, 0), ("O", 1, 0),
    ("O", 0, 0), ("O", 3, 0), ("C", 2, 0), ("O", 2, 1), ("O", 3, 1), ("O", 0, 1), ("E", 2, 1), ("O", 1, 1),
    ("E", 1, 1), ("C", 2, 1), ("L", 2, 1), ("L", 1, 1), ("C", 0, 1), ("C", 1, 1), ("tot",),
)


class Place:
    def __init__(self):
        row, col = lax.axis_index("row"), lax.axis_index("col")
        self.row, self.col = row, col
        self.yl, self.z, self.x = row // 16, (row // 4) % 4, row % 4
        self.yh, self.c = col // 2, col % 2

    def dev(self, x=None, z=None, yl=None, yh=None, c=None):
        x = self.x if x is None else x
        z = self.z if z is None else z
        yl = self.yl if yl is None else yl
        yh = self.yh if yh is None else yh
        c = self.c if c is None else c
        return (yl * 16 + z * 4 + x, yh * 2 + c)


class Copies:
    def __init__(self, send_sem, recv_sem, me):
        self.send_sem, self.recv_sem, self.me = send_sem, recv_sem, me
        self.ids, self.sent, self.met = {}, [], set()

    def slot(self, name):
        return self.ids.setdefault(name, len(self.ids))

    def make(self, name, src, dst, dev):
        k = self.slot(name)
        return pltpu.make_async_remote_copy(
            src_ref=src, dst_ref=dst, send_sem=self.send_sem.at[k], recv_sem=self.recv_sem.at[k],
            device_id=dev, device_id_type=MESH)

    def send(self, name, src, dst, dev):
        copy = self.make(name, src, dst, dev)
        copy.start()
        self.sent.append(copy)

    def wait(self, name, landed, dev):
        self.make(name, landed, landed, dev).wait_recv()

    def need(self, name, landed, dev):
        if name not in self.met:
            self.met.add(name)
            self.wait(name, landed, dev)

    def drain(self):
        for copy in self.sent:
            copy.wait_send()


def kernel(tile, flow_hbm, pattern_hbm, keep_hbm, q_out, gs_out, flow, pattern, keep, a, b, m, araw, yraw, xraw, craw, c, cq,
           xs, zs, inv, kx, km, ts, gsend, gs, send_sem, recv_sem, local_sem):
    me = Place()
    rows, cols = flow.shape
    nt = cols // tile
    half = rows // 2
    wide = cols // 4
    side = wide // 2
    ring = RING * rows // 8
    parts = ((0, ring // 2), (ring // 2, ring // 2), (ring, rows - ring))
    x, z, yl, yh, core = me.x, me.z, me.yl, me.yh, me.c
    net = Copies(send_sem, recv_sem, me)
    zp, zm, z2 = (z + 1) % 4, (z + 3) % 4, (z + 2) % 4
    xp, xm, x2 = (x + 1) % 4, (x + 3) % 4, (x + 2) % 4
    around = [(d, dy) for dy in (0, 1) for d in range(4) if (d, dy) != (0, 0)]
    mate, across, beside = me.dev(c=1 - core), me.dev(yh=1 - yh), me.dev(yl=1 - yl)
    fetch = [pltpu.make_async_copy(src, dst, local_sem.at[k])
             for k, (src, dst) in enumerate(((flow_hbm, flow), (pattern_hbm, pattern), (keep_hbm, keep)))]
    for copy in fetch:
        copy.start()
    barrier = pltpu.get_barrier_semaphore()
    peers = ([me.dev(x=(x + d) % 4, yl=(yl + dy) % 2) for d, dy in around]
             + [me.dev(z=(z + d) % 4, yl=(yl + dy) % 2) for d, dy in around if d] + [mate, across])
    for dev in peers:
        pl.semaphore_signal(barrier, inc=1, device_id=dev, device_id_type=MESH)

    q0, q1 = yh * 2 + core, (1 - yh) * 2 + core
    z_mates = (z, zm, zp, z2)
    z_order = (z, zp, zm, z2)
    pieces = [(yl, zz) for zz in z_order] + [(1 - yl, zz) for zz in z_order]

    def block(yy, zz, xx):
        return yy * 16 + zz * 4 + xx

    def a_at(q, k, start=0, size=rows):
        return a.at[q, pl.ds(k * rows + start, size)]

    def b_at(n, yy, zz, xx, start=0, size=rows):
        return b.at[n, pl.ds(pl.multiple_of(block(yy, zz, xx) * rows + start, half), size)]

    def chunk(ref, j):
        return ref.at[:, pl.ds(pl.multiple_of(j * wide, wide), wide)]

    def half_chunk(ref, j, n):
        return ref.at[:, pl.ds(pl.multiple_of(j * wide + n * side, side), side)]

    def eye(count, first_row, first_col):
        r = lax.broadcasted_iota(jnp.int32, (count, tile), 0)
        k = lax.broadcasted_iota(jnp.int32, (count, tile), 1)
        return (r - k == first_col - first_row).astype(F32)

    def normalise(dst, src, masses, count, first_row, col, first_tile):
        height = src.shape[0]

        def step(t, _):
            at = pl.ds(pl.multiple_of(t * tile, tile), tile)
            there = pl.ds(pl.multiple_of((first_tile + t) * tile, tile), tile)
            value = src[:, at].astype(F32) + eye(height, first_row, col * cols + (first_tile + t) * tile)
            dst[:, at] = (value * inv[masses, :, there]).astype(BF16)
            return _

        lax.fori_loop(0, count, step, 0)

    def normalise_b(n, yy, zz, xx, src):
        count = side // tile
        normalise(b_at(n, yy, zz, xx), src, 0, count, block(yy, zz, xx) * rows, me.col, (2 * z + n) * count)

    def normalise_a(k, src):
        normalise(a_at(q0, k), src, 0, nt, block(yl, z_mates[k], x) * rows, me.col, 0)

    def landed_x(i, n, k, start=0, size=rows):
        if i == 0:
            return xraw.at[k, n, pl.ds(start, size)]
        yy, zz = pieces[i]
        return b_at(n, yy, zz, (xm, xp, x2)[k], start, size)

    def sent_x(i, n, k, start=0, size=rows):
        if i == 0:
            return xraw.at[k, n, pl.ds(start, size)]
        yy, zz = pieces[i]
        return b_at(n, yy, zz, x if k < 2 else (xm if start == 0 else xp), start, size)

    def spread_x(i, n, src):
        net.send(("bx+", i, n), src, sent_x(i, n, 0), me.dev(x=xp))
        net.send(("bx-", i, n), src, sent_x(i, n, 1), me.dev(x=xm))

    def forward_x(i, n):
        net.wait(("bx+", i, n), landed_x(i, n, 0), me.dev(x=xm))
        net.send(("bf+", i, n), landed_x(i, n, 0, 0, half), sent_x(i, n, 2, 0, half), me.dev(x=xp))
        net.wait(("bx-", i, n), landed_x(i, n, 1), me.dev(x=xp))
        net.send(("bf-", i, n), landed_x(i, n, 1, half, half), sent_x(i, n, 2, half, half), me.dev(x=xm))

    def last_x(i, n):
        net.need(("bf+", i, n), landed_x(i, n, 2, 0, half), me.dev(x=xm))
        net.need(("bf-", i, n), landed_x(i, n, 2, half, half), me.dev(x=xp))

    def start():
        for copy in fetch:
            copy.wait()
        for t in range(nt):
            at = slice(t * tile, (t + 1) * tile)
            on = (pattern[0, t] > 0).astype(F32)
            masked = flow[:, at].astype(F32) * on
            m[:, at] = masked.astype(BF16)
            diagonal = me.row == me.col * nt + t
            xs[x, :, at] = jnp.sum(masked, axis=0, keepdims=True) + diagonal.astype(F32)
            kept = jnp.logical_or(keep[0, t] > 0, diagonal).astype(F32)
            kx[:, at] = jnp.broadcast_to(kept, (8, tile))
        km[z] = kx[:, pl.ds(pl.multiple_of(z * wide, wide), wide)]
        ts[yl * 4 + x] = jnp.zeros(ts.shape[1:], F32)
        pl.semaphore_wait(barrier, len(peers))
        for d in (1, 3, 2):
            net.send(("mx", d), xs.at[x], xs.at[x], me.dev(x=(x + d) % 4))
        send_z0(0)
        for n in (0, 1):
            spread_x(0, n, half_chunk(m, z, n))

    def masses_x():
        for d in (1, 3, 2):
            src = (x - d + 4) % 4
            net.wait(("mx", d), xs.at[src], me.dev(x=src))
        here = yl * 4 + z
        zs[here] = (xs[0] + xs[1]) + (xs[2] + xs[3])
        for d, dy in around:
            net.send(("mz", d, dy), zs.at[here], zs.at[here], me.dev(z=(z + d) % 4, yl=(yl + dy) % 2))
        for d in (1, 3, 2):
            net.send(("k", d), chunk(kx, (z + d) % 4), km.at[z], me.dev(z=(z + d) % 4))
        send_z0(1)

    def send_y(p):
        at = pl.ds(parts[p][0], parts[p][1])
        net.send(("ay", p), m.at[at], yraw.at[at], across)

    def send_b(n):
        net.send(("by", 0, n), half_chunk(m, z, n), craw.at[n], beside)

    def masses_z():
        for d, dy in around:
            zz, yy = (z - d + 4) % 4, (yl + dy) % 2
            net.wait(("mz", d, dy), zs.at[yy * 4 + zz], me.dev(z=zz, yl=yy))
        mass = ((zs[0] + zs[1]) + (zs[2] + zs[3])) + ((zs[4] + zs[5]) + (zs[6] + zs[7]))
        inv[0] = 1.0 / mass
        net.send("iv", inv.at[0], inv.at[1], across)

    def home(i, n):
        yy, zz = pieces[i]
        piece = b_at(n, yy, zz, x)
        if i < 4:
            k = {1: 1, 2: 0, 3: 2}[i]
            if k < 2:
                take_z0(k, 0)
            else:
                last_z0(0)
            normalise_b(n, yy, zz, x, half_chunk(araw.at[k], z, n))
            net.send(("by", i, n), piece, piece, beside)
        else:
            net.wait(("by", i - 4, n), craw.at[n] if i == 4 else piece, beside)
            if i == 4:
                normalise_b(n, yy, zz, x, craw.at[n])
        spread_x(i, n, piece)

    def own_a():
        normalise_a(0, m)
        net.send(("ac0", 0), a_at(q0, 0), a_at(q0, 0), mate)

    def own_b():
        for n in (0, 1):
            normalise_b(n, yl, z, x, half_chunk(m, z, n))
        c[...] = jnp.zeros(c.shape, F32)

    def raw_x(n):
        last_x(0, n)
        for k, xx in enumerate((xm, xp, x2)):
            normalise_b(n, yl, z, xx, xraw.at[k, n])

    plus, minus = (zp, z2, z, zm), (zm, z2, z, zp)

    def send_z0(n):
        net.send(("az0+", n), chunk(m, plus[n]), chunk(araw.at[0], plus[n]), me.dev(z=zp))
        net.send(("az0-", n), chunk(m, minus[n]), chunk(araw.at[1], minus[n]), me.dev(z=zm))

    def take_z0(k, n):
        if k == 0:
            net.need(("az0+", n), chunk(araw.at[0], (z, zp, zm, z2)[n]), me.dev(z=zm))
        else:
            net.need(("az0-", n), chunk(araw.at[1], (z, zm, zp, z2)[n]), me.dev(z=zp))

    def rows_of(ref, h):
        return ref.at[pl.ds(h * half, half)]

    def forward_z0(n):
        take_z0(0, n)
        j = (z, zp, zm, z2)[n]
        net.send(("af0+", n), rows_of(chunk(araw.at[0], j), 0), rows_of(chunk(araw.at[2], j), 0), me.dev(z=zp))
        take_z0(1, n)
        j = (z, zm, zp, z2)[n]
        net.send(("af0-", n), rows_of(chunk(araw.at[1], j), 1), rows_of(chunk(araw.at[2], j), 1), me.dev(z=zm))

    def last_z0(f):
        n = (1, 0, 2, 3)[f]
        net.need(("af0+", n), rows_of(chunk(araw.at[2], (zm, z, z2, zp)[n]), 0), me.dev(z=zm))
        net.need(("af0-", n), rows_of(chunk(araw.at[2], (zp, z, z2, zm)[n]), 1), me.dev(z=zp))

    def finish_z0(k):
        for n in range(4):
            if k == 2:
                last_z0(n)
            else:
                take_z0(k, n)
        normalise_a(k + 1, araw.at[k])
        rest = a_at(q0, k + 1, *parts[2])
        net.send(("ar", k), rest, rest, across)
        net.send(("ac0", k + 1), a_at(q0, k + 1), a_at(q0, k + 1), mate)

    def to_mate(k, p):
        net.send(("ac1", k, p), a_at(q1, k, *parts[p]), a_at(q1, k, *parts[p]), mate)

    def take_y(p):
        at = a_at(q1, 0, *parts[p])
        first, size = parts[p]
        raw = yraw.at[pl.ds(first, size)]
        net.wait(("ay", p), raw, across)
        net.need("iv", inv.at[1], across)
        normalise(at, raw, 1, nt, block(yl, z, x) * rows + first, q1, 0)
        if p < 2:
            net.send(("az1+", p), at, a_at(q1, 1, *parts[p]), me.dev(z=zp))
            net.send(("az1-", p), at, a_at(q1, 2, *parts[p]), me.dev(z=zm))
        to_mate(0, p)

    def take_rest(k):
        net.wait(("ar", k), a_at(q1, k + 1, *parts[2]), across)
        to_mate(k + 1, 2)

    def sub(k, p, side_of):
        first, size = parts[p]
        upper = (size // 2 + 15) // 16 * 16
        return a_at(q1, k, first, upper) if side_of == 0 else a_at(q1, k, first + upper, size - upper)

    def take_z1(p):
        net.wait(("az1+", p), a_at(q1, 1, *parts[p]), me.dev(z=zm))
        net.send(("af1+", p), sub(1, p, 0), sub(3, p, 0), me.dev(z=zp))
        net.wait(("az1-", p), a_at(q1, 2, *parts[p]), me.dev(z=zp))
        net.send(("af1-", p), sub(2, p, 1), sub(3, p, 1), me.dev(z=zm))
        to_mate(1, p)
        to_mate(2, p)

    def opposite_z1(p):
        net.wait(("af1+", p), sub(3, p, 0), me.dev(z=zm))
        net.wait(("af1-", p), sub(3, p, 1), me.dev(z=zp))
        to_mate(3, p)

    def ready_b(j, n):
        last_x(j, n)
        last_x(j + 4, n)

    def mate0():
        for k in range(4):
            net.need(("ac0", k), a_at(yh * 2 + 1 - core, k), mate)

    def mate1(k):
        for p in (0, 1, 2):
            net.need(("ac1", k, p), a_at((1 - yh) * 2 + 1 - core, k, *parts[p]), mate)

    def units(yy, piece, n, first, count):
        zi = z_order[piece]
        deep = 4 * rows
        left = a[yy * 2 + zi // 2, pl.ds(first * rows, count * rows), pl.ds(pl.multiple_of((zi % 2) * deep, deep), deep)]
        right = b[n, pl.ds(pl.multiple_of((yy * 4 + zi) * deep, deep), deep)]
        c[pl.ds(first * rows, count * rows), n * side:(n + 1) * side] += jnp.dot(left, right, preferred_element_type=F32)

    def early(j, n):
        mate0()
        ready_b(j, n)
        units(yh, j, n, 0, 4)

    def late(j, n, first, count):
        for k in range(first, first + count):
            mate1(k)
        ready_b(j, n)
        units(1 - yh, j, n, first, count)

    mine = yl * 4 + x

    def finish(d, n):
        zz = (z + d) % 4
        if d:
            net.need(("k", (4 - d) % 4), km.at[zz], me.dev(z=zz))
        slot = (0, 2, 3, 1)[d]
        at = slice(n * side, (n + 1) * side)
        kept = c[slot * rows:(slot + 1) * rows, at] * km[zz, 0:1, at]
        ts[mine, :, at] += jnp.sum(kept * kept, axis=0, keepdims=True)
        top = jnp.max(kept, axis=0, keepdims=True)
        up = jnp.where(top > 0, 32767.0 / jnp.where(top > 0, top, 1.0), 0.0)
        cq[d, n] = jnp.round(kept * up).astype(jnp.int32).astype(jnp.int16)
        gsend[d, :, at] = top * (1.0 / 32767.0)
        if d:
            net.send(("c", d, n), cq.at[d, n], half_chunk(q_out, z, n), me.dev(z=zz))

    def finish_step(k, n):
        for d in ((0,), (1, 3), (2,))[k]:
            finish(d, n)

    def total():
        own = [pltpu.make_async_copy(cq.at[0, n], half_chunk(q_out, z, n), local_sem.at[n]) for n in (0, 1)]
        for copy in own:
            copy.start()
        for d, dy in around:
            net.send(("t", d, dy), ts.at[mine], ts.at[mine], me.dev(x=(x + d) % 4, yl=(yl + dy) % 2))
        for d, dy in around:
            xx, yy = (x - d + 4) % 4, (yl + dy) % 2
            net.wait(("t", d, dy), ts.at[yy * 4 + xx], me.dev(x=xx, yl=yy))
        whole = ((ts[0] + ts[1]) + (ts[2] + ts[3])) + ((ts[4] + ts[5]) + (ts[6] + ts[7]))
        scale = (rows * 32) / whole
        for d in range(4):
            gsend[d, :, wide:] = scale
        gs[z] = gsend[0]
        for d in (1, 3, 2):
            net.send(("s", d), gsend.at[d], gs.at[z], me.dev(z=(z + d) % 4))
        for copy in own:
            copy.wait()
        for d in (1, 3, 2):
            src = (z - d + 4) % 4
            net.wait(("s", d), gs.at[src], me.dev(z=src))
        gs_out[...] = gs[...]
        for d in (1, 3, 2):
            src = (z - d + 4) % 4
            for n in (0, 1):
                net.wait(("c", d, n), half_chunk(q_out, src, n), me.dev(z=src))
        net.drain()

    steps = {"start": start, "mx": masses_x, "inv": masses_z, "own": own_a, "nb0": own_b, "z1": take_z1, "zo": opposite_z1,
             "tot": total, "home": home, "f": forward_x, "lx": raw_x, "sy": send_y, "sb": send_b, "sa": send_z0,
             "g": forward_z0, "y": take_y, "fin": finish_z0, "r": take_rest, "E": early, "C": finish_step,
             "L": lambda j, n: late(j, n, 0, 3), "O": lambda j, n: late(j, n, 3, 1)}
    for name, *which in ORDER:
        steps[name](*which)


def body(flow, pattern, keep):
    rows, cols = flow.shape
    tile = cols // pattern.shape[1]
    wide = cols // 4
    side = wide // 2
    vmem = pl.BlockSpec(memory_space=pltpu.VMEM)
    anyspace = pl.BlockSpec(memory_space=pl.ANY)
    messages = 152
    coded, factors = pl.pallas_call(
        lambda *refs: kernel(tile, *refs),
        out_shape=(jax.ShapeDtypeStruct((rows, cols), jnp.int16), jax.ShapeDtypeStruct((4, 1, 2 * wide), F32)),
        in_specs=[pl.BlockSpec(memory_space=pltpu.HBM)] * 3,
        out_specs=(anyspace, vmem),
        scratch_shapes=[
            pltpu.VMEM((rows, cols), BF16),
            pltpu.SMEM(pattern.shape, jnp.int32),
            pltpu.SMEM(keep.shape, jnp.int32),
            pltpu.VMEM((4, 4 * rows, cols), BF16),
            pltpu.VMEM((2, 32 * rows, side), BF16),
            pltpu.VMEM((rows, cols), BF16),
            pltpu.VMEM((3, rows, cols), BF16),
            pltpu.VMEM((rows, cols), BF16),
            pltpu.VMEM((3, 2, rows, side), BF16),
            pltpu.VMEM((2, rows, side), BF16),
            pltpu.VMEM((4 * rows, wide), F32),
            pltpu.VMEM((4, 2, rows, side), jnp.int16),
            pltpu.VMEM((4, 1, cols), F32),
            pltpu.VMEM((8, 1, cols), F32),
            pltpu.VMEM((2, 1, cols), F32),
            pltpu.VMEM((8, cols), F32),
            pltpu.VMEM((4, 8, wide), F32),
            pltpu.VMEM((8, 1, wide), F32),
            pltpu.VMEM((4, 1, 2 * wide), F32),
            pltpu.VMEM((4, 1, 2 * wide), F32),
            pltpu.SemaphoreType.DMA((messages,)),
            pltpu.SemaphoreType.DMA((messages,)),
            pltpu.SemaphoreType.DMA((3,)),
        ],
        compiler_params=pltpu.CompilerParams(
            collective_id=0, has_side_effects=True, vmem_limit_bytes=52000 * 1024),
        name="cluster",
    )(*(pltpu.with_memory_space_constraint(v, pltpu.HBM) for v in (flow, pattern, keep)))
    down = factors[:, 0, :wide].reshape(1, cols)
    scale = factors[:, 0, wide:].reshape(1, cols)
    expanded = coded.astype(F32) * down
    return expanded * expanded * scale


def solution(mesh):
    return jax.shard_map(
        body,
        mesh=mesh,
        in_specs=(P("row", "col"), P("row", "col"), P("row", "col")),
        out_specs=P("row", "col"),
        check_vma=False,
    )
```

```python
import jax
import jax.numpy as jnp
from jax import lax
from jax.experimental import pallas as pl
from jax.experimental.pallas import tpu as pltpu
from jax.sharding import PartitionSpec as P

MESH = pl.DeviceIdType.MESH
F32 = jnp.float32
BF16 = jnp.bfloat16
RING = 7
ORDER = (
    ("start",), ("mx",), ("sa", 2), ("sb", 0), ("f", 0, 0), ("sb", 1), ("f", 0, 1), ("inv",), ("home", 2, 0),
    ("home", 4, 0), ("home", 1, 1), ("sy", 1), ("g", 1), ("sa", 3), ("nb0",), ("home", 4, 1), ("sy", 0), ("own",),
    ("f", 4, 0), ("g", 2), ("lx", 0), ("home", 6, 0), ("lx", 1), ("home", 1, 0), ("home", 3, 0), ("g", 0),
    ("f", 2, 0), ("g", 3), ("sy", 2), ("home", 5, 1), ("fin", 1), ("y", 1), ("home", 2, 1), ("f", 1, 1), ("fin", 0),
    ("f", 4, 1), ("fin", 2), ("f", 1, 0), ("y", 0), ("home", 5, 0), ("f", 3, 0), ("f", 6, 0), ("f", 5, 0), ("y", 2),
    ("home", 7, 0), ("z1", 1), ("E", 2, 0), ("f", 5, 1), ("r", 1), ("home", 6, 1), ("E", 0, 1), ("z1", 0),
    ("f", 7, 0), ("E", 1, 0), ("home", 3, 1), ("E", 1, 1), ("E", 0, 0), ("r", 0), ("f", 2, 1), ("f", 6, 1),
    ("E", 3, 0), ("r", 2), ("zo", 1), ("L", 0, 0), ("home", 7, 1), ("L", 3, 0), ("L", 2, 0), ("L", 1, 0), ("f", 3, 1),
    ("zo", 0), ("C", 1, 0), ("L", 1, 1), ("E", 2, 1), ("L", 0, 1), ("f", 7, 1), ("C", 0, 0), ("L", 2, 1), ("O", 0, 0),
    ("O", 1, 0), ("O", 3, 0), ("O", 2, 0), ("C", 2, 0), ("O", 2, 1), ("O", 0, 1), ("E", 3, 1), ("L", 3, 1),
    ("C", 1, 1), ("O", 3, 1), ("O", 1, 1), ("C", 2, 1), ("C", 0, 1), ("tot",),
)


class Place:
    def __init__(self):
        row, col = lax.axis_index("row"), lax.axis_index("col")
        self.row, self.col = row, col
        self.yl, self.z, self.x = row // 16, (row // 4) % 4, row % 4
        self.yh, self.c = col // 2, col % 2

    def dev(self, x=None, z=None, yl=None, yh=None, c=None):
        x = self.x if x is None else x
        z = self.z if z is None else z
        yl = self.yl if yl is None else yl
        yh = self.yh if yh is None else yh
        c = self.c if c is None else c
        return (yl * 16 + z * 4 + x, yh * 2 + c)


class Copies:
    def __init__(self, send_sem, recv_sem, me):
        self.send_sem, self.recv_sem, self.me = send_sem, recv_sem, me
        self.ids, self.sent, self.met = {}, [], set()

    def slot(self, name):
        return self.ids.setdefault(name, len(self.ids))

    def make(self, name, src, dst, dev):
        k = self.slot(name)
        return pltpu.make_async_remote_copy(
            src_ref=src, dst_ref=dst, send_sem=self.send_sem.at[k], recv_sem=self.recv_sem.at[k],
            device_id=dev, device_id_type=MESH)

    def send(self, name, src, dst, dev):
        copy = self.make(name, src, dst, dev)
        copy.start()
        self.sent.append(copy)

    def wait(self, name, landed, dev):
        self.make(name, landed, landed, dev).wait_recv()

    def need(self, name, landed, dev):
        if name not in self.met:
            self.met.add(name)
            self.wait(name, landed, dev)

    def drain(self):
        for copy in self.sent:
            copy.wait_send()


def kernel(tile, flow_hbm, pattern_hbm, keep_hbm, q_out, gs_out, flow, pattern, keep, a, b, m, araw, yraw, xraw, craw, c, cq,
           xs, zs, inv, kx, km, ts, gsend, gs, send_sem, recv_sem, local_sem):
    me = Place()
    rows, cols = flow.shape
    nt = cols // tile
    half = rows // 2
    wide = cols // 4
    side = wide // 2
    ring = RING * rows // 8
    parts = ((0, ring // 2), (ring // 2, ring // 2), (ring, rows - ring))
    x, z, yl, yh, core = me.x, me.z, me.yl, me.yh, me.c
    net = Copies(send_sem, recv_sem, me)
    zp, zm, z2 = (z + 1) % 4, (z + 3) % 4, (z + 2) % 4
    xp, xm, x2 = (x + 1) % 4, (x + 3) % 4, (x + 2) % 4
    around = [(d, dy) for dy in (0, 1) for d in range(4) if (d, dy) != (0, 0)]
    mate, across, beside = me.dev(c=1 - core), me.dev(yh=1 - yh), me.dev(yl=1 - yl)
    fetch = [pltpu.make_async_copy(src, dst, local_sem.at[k])
             for k, (src, dst) in enumerate(((flow_hbm, flow), (pattern_hbm, pattern), (keep_hbm, keep)))]
    for copy in fetch:
        copy.start()
    barrier = pltpu.get_barrier_semaphore()
    peers = ([me.dev(x=(x + d) % 4, yl=(yl + dy) % 2) for d, dy in around]
             + [me.dev(z=(z + d) % 4, yl=(yl + dy) % 2) for d, dy in around if d] + [mate, across])
    for dev in peers:
        pl.semaphore_signal(barrier, inc=1, device_id=dev, device_id_type=MESH)

    q0, q1 = yh * 2 + core, (1 - yh) * 2 + core
    z_mates = (z, zm, zp, z2)
    z_order = (z, zp, zm, z2)
    pieces = [(yl, zz) for zz in z_order] + [(1 - yl, zz) for zz in z_order]

    def block(yy, zz, xx):
        return yy * 16 + zz * 4 + xx

    def a_at(q, k, start=0, size=rows):
        return a.at[q, pl.ds(k * rows + start, size)]

    def b_at(n, yy, zz, xx, start=0, size=rows):
        return b.at[n, pl.ds(pl.multiple_of(block(yy, zz, xx) * rows + start, half), size)]

    def chunk(ref, j):
        return ref.at[:, pl.ds(pl.multiple_of(j * wide, wide), wide)]

    def half_chunk(ref, j, n):
        return ref.at[:, pl.ds(pl.multiple_of(j * wide + n * side, side), side)]

    def eye(count, first_row, first_col):
        r = lax.broadcasted_iota(jnp.int32, (count, tile), 0)
        k = lax.broadcasted_iota(jnp.int32, (count, tile), 1)
        return (r - k == first_col - first_row).astype(F32)

    def normalise(dst, src, masses, count, first_row, col, first_tile):
        height = src.shape[0]

        def step(t, _):
            at = pl.ds(pl.multiple_of(t * tile, tile), tile)
            there = pl.ds(pl.multiple_of((first_tile + t) * tile, tile), tile)
            value = src[:, at].astype(F32) + eye(height, first_row, col * cols + (first_tile + t) * tile)
            dst[:, at] = (value * inv[masses, :, there]).astype(BF16)
            return _

        lax.fori_loop(0, count, step, 0)

    def normalise_b(n, yy, zz, xx, src):
        count = side // tile
        normalise(b_at(n, yy, zz, xx), src, 0, count, block(yy, zz, xx) * rows, me.col, (2 * z + n) * count)

    def normalise_a(k, src):
        normalise(a_at(q0, k), src, 0, nt, block(yl, z_mates[k], x) * rows, me.col, 0)

    def landed_x(i, n, k, start=0, size=rows):
        if i == 0:
            return xraw.at[k, n, pl.ds(start, size)]
        yy, zz = pieces[i]
        return b_at(n, yy, zz, (xm, xp, x2)[k], start, size)

    def sent_x(i, n, k, start=0, size=rows):
        if i == 0:
            return xraw.at[k, n, pl.ds(start, size)]
        yy, zz = pieces[i]
        return b_at(n, yy, zz, x if k < 2 else (xm if start == 0 else xp), start, size)

    def spread_x(i, n, src):
        net.send(("bx+", i, n), src, sent_x(i, n, 0), me.dev(x=xp))
        net.send(("bx-", i, n), src, sent_x(i, n, 1), me.dev(x=xm))

    def forward_x(i, n):
        net.wait(("bx+", i, n), landed_x(i, n, 0), me.dev(x=xm))
        net.send(("bf+", i, n), landed_x(i, n, 0, 0, half), sent_x(i, n, 2, 0, half), me.dev(x=xp))
        net.wait(("bx-", i, n), landed_x(i, n, 1), me.dev(x=xp))
        net.send(("bf-", i, n), landed_x(i, n, 1, half, half), sent_x(i, n, 2, half, half), me.dev(x=xm))

    def last_x(i, n):
        net.need(("bf+", i, n), landed_x(i, n, 2, 0, half), me.dev(x=xm))
        net.need(("bf-", i, n), landed_x(i, n, 2, half, half), me.dev(x=xp))

    def start():
        for copy in fetch:
            copy.wait()
        for t in range(nt):
            at = slice(t * tile, (t + 1) * tile)
            on = (pattern[0, t] > 0).astype(F32)
            masked = flow[:, at].astype(F32) * on
            m[:, at] = masked.astype(BF16)
            diagonal = me.row == me.col * nt + t
            xs[x, :, at] = jnp.sum(masked, axis=0, keepdims=True) + diagonal.astype(F32)
            kept = jnp.logical_or(keep[0, t] > 0, diagonal).astype(F32)
            kx[:, at] = jnp.broadcast_to(kept, (8, tile))
        km[z] = kx[:, pl.ds(pl.multiple_of(z * wide, wide), wide)]
        ts[yl * 4 + x] = jnp.zeros(ts.shape[1:], F32)
        pl.semaphore_wait(barrier, len(peers))
        for d in (1, 3, 2):
            net.send(("mx", d), xs.at[x], xs.at[x], me.dev(x=(x + d) % 4))
        send_z0(0)
        for n in (0, 1):
            spread_x(0, n, half_chunk(m, z, n))

    def masses_x():
        for d in (1, 3, 2):
            src = (x - d + 4) % 4
            net.wait(("mx", d), xs.at[src], me.dev(x=src))
        here = yl * 4 + z
        zs[here] = (xs[0] + xs[1]) + (xs[2] + xs[3])
        for d, dy in around:
            net.send(("mz", d, dy), zs.at[here], zs.at[here], me.dev(z=(z + d) % 4, yl=(yl + dy) % 2))
        for d in (1, 3, 2):
            net.send(("k", d), chunk(kx, (z + d) % 4), km.at[z], me.dev(z=(z + d) % 4))
        send_z0(1)

    def send_y(p):
        at = pl.ds(parts[p][0], parts[p][1])
        net.send(("ay", p), m.at[at], yraw.at[at], across)

    def send_b(n):
        net.send(("by", 0, n), half_chunk(m, z, n), craw.at[n], beside)

    def masses_z():
        for d, dy in around:
            zz, yy = (z - d + 4) % 4, (yl + dy) % 2
            net.wait(("mz", d, dy), zs.at[yy * 4 + zz], me.dev(z=zz, yl=yy))
        mass = ((zs[0] + zs[1]) + (zs[2] + zs[3])) + ((zs[4] + zs[5]) + (zs[6] + zs[7]))
        inv[0] = 1.0 / mass
        net.send("iv", inv.at[0], inv.at[1], across)

    def home(i, n):
        yy, zz = pieces[i]
        piece = b_at(n, yy, zz, x)
        if i < 4:
            k = {1: 1, 2: 0, 3: 2}[i]
            if k < 2:
                take_z0(k, 0)
            else:
                last_z0(0)
            normalise_b(n, yy, zz, x, half_chunk(araw.at[k], z, n))
            net.send(("by", i, n), piece, piece, beside)
        else:
            net.wait(("by", i - 4, n), craw.at[n] if i == 4 else piece, beside)
            if i == 4:
                normalise_b(n, yy, zz, x, craw.at[n])
        spread_x(i, n, piece)

    def own_a():
        normalise_a(0, m)
        net.send(("ac0", 0), a_at(q0, 0), a_at(q0, 0), mate)

    def own_b():
        for n in (0, 1):
            normalise_b(n, yl, z, x, half_chunk(m, z, n))
        c[...] = jnp.zeros(c.shape, F32)

    def raw_x(n):
        last_x(0, n)
        for k, xx in enumerate((xm, xp, x2)):
            normalise_b(n, yl, z, xx, xraw.at[k, n])

    plus, minus = (zp, z2, z, zm), (zm, z2, z, zp)

    def send_z0(n):
        net.send(("az0+", n), chunk(m, plus[n]), chunk(araw.at[0], plus[n]), me.dev(z=zp))
        net.send(("az0-", n), chunk(m, minus[n]), chunk(araw.at[1], minus[n]), me.dev(z=zm))

    def take_z0(k, n):
        if k == 0:
            net.need(("az0+", n), chunk(araw.at[0], (z, zp, zm, z2)[n]), me.dev(z=zm))
        else:
            net.need(("az0-", n), chunk(araw.at[1], (z, zm, zp, z2)[n]), me.dev(z=zp))

    def rows_of(ref, h):
        return ref.at[pl.ds(h * half, half)]

    def forward_z0(n):
        take_z0(0, n)
        j = (z, zp, zm, z2)[n]
        net.send(("af0+", n), rows_of(chunk(araw.at[0], j), 0), rows_of(chunk(araw.at[2], j), 0), me.dev(z=zp))
        take_z0(1, n)
        j = (z, zm, zp, z2)[n]
        net.send(("af0-", n), rows_of(chunk(araw.at[1], j), 1), rows_of(chunk(araw.at[2], j), 1), me.dev(z=zm))

    def last_z0(f):
        n = (1, 0, 2, 3)[f]
        net.need(("af0+", n), rows_of(chunk(araw.at[2], (zm, z, z2, zp)[n]), 0), me.dev(z=zm))
        net.need(("af0-", n), rows_of(chunk(araw.at[2], (zp, z, z2, zm)[n]), 1), me.dev(z=zp))

    def finish_z0(k):
        for n in range(4):
            if k == 2:
                last_z0(n)
            else:
                take_z0(k, n)
        normalise_a(k + 1, araw.at[k])
        rest = a_at(q0, k + 1, *parts[2])
        net.send(("ar", k), rest, rest, across)
        net.send(("ac0", k + 1), a_at(q0, k + 1), a_at(q0, k + 1), mate)

    def to_mate(k, p):
        net.send(("ac1", k, p), a_at(q1, k, *parts[p]), a_at(q1, k, *parts[p]), mate)

    def take_y(p):
        at = a_at(q1, 0, *parts[p])
        first, size = parts[p]
        raw = yraw.at[pl.ds(first, size)]
        net.wait(("ay", p), raw, across)
        net.need("iv", inv.at[1], across)
        normalise(at, raw, 1, nt, block(yl, z, x) * rows + first, q1, 0)
        if p < 2:
            net.send(("az1+", p), at, a_at(q1, 1, *parts[p]), me.dev(z=zp))
            net.send(("az1-", p), at, a_at(q1, 2, *parts[p]), me.dev(z=zm))
        to_mate(0, p)

    def take_rest(k):
        net.wait(("ar", k), a_at(q1, k + 1, *parts[2]), across)
        to_mate(k + 1, 2)

    def sub(k, p, side_of):
        first, size = parts[p]
        upper = (size // 2 + 15) // 16 * 16
        return a_at(q1, k, first, upper) if side_of == 0 else a_at(q1, k, first + upper, size - upper)

    def take_z1(p):
        net.wait(("az1+", p), a_at(q1, 1, *parts[p]), me.dev(z=zm))
        net.send(("af1+", p), sub(1, p, 0), sub(3, p, 0), me.dev(z=zp))
        net.wait(("az1-", p), a_at(q1, 2, *parts[p]), me.dev(z=zp))
        net.send(("af1-", p), sub(2, p, 1), sub(3, p, 1), me.dev(z=zm))
        to_mate(1, p)
        to_mate(2, p)

    def opposite_z1(p):
        net.wait(("af1+", p), sub(3, p, 0), me.dev(z=zm))
        net.wait(("af1-", p), sub(3, p, 1), me.dev(z=zp))
        to_mate(3, p)

    def ready_b(j, n):
        last_x(j, n)
        last_x(j + 4, n)

    def mate0():
        for k in range(4):
            net.need(("ac0", k), a_at(yh * 2 + 1 - core, k), mate)

    def mate1(k):
        for p in (0, 1, 2):
            net.need(("ac1", k, p), a_at((1 - yh) * 2 + 1 - core, k, *parts[p]), mate)

    def units(yy, piece, n, first, count):
        zi = z_order[piece]
        deep = 4 * rows
        left = a[yy * 2 + zi // 2, pl.ds(first * rows, count * rows), pl.ds(pl.multiple_of((zi % 2) * deep, deep), deep)]
        right = b[n, pl.ds(pl.multiple_of((yy * 4 + zi) * deep, deep), deep)]
        c[pl.ds(first * rows, count * rows), n * side:(n + 1) * side] += jnp.dot(left, right, preferred_element_type=F32)

    def early(j, n):
        mate0()
        ready_b(j, n)
        units(yh, j, n, 0, 4)

    def late(j, n, first, count):
        for k in range(first, first + count):
            mate1(k)
        ready_b(j, n)
        units(1 - yh, j, n, first, count)

    mine = yl * 4 + x

    def finish(d, n):
        zz = (z + d) % 4
        if d:
            net.need(("k", (4 - d) % 4), km.at[zz], me.dev(z=zz))
        slot = (0, 2, 3, 1)[d]
        at = slice(n * side, (n + 1) * side)
        kept = c[slot * rows:(slot + 1) * rows, at] * km[zz, 0:1, at]
        ts[mine, :, at] += jnp.sum(kept * kept, axis=0, keepdims=True)
        top = jnp.max(kept, axis=0, keepdims=True)
        up = jnp.where(top > 0, 32767.0 / jnp.where(top > 0, top, 1.0), 0.0)
        cq[d, n] = jnp.round(kept * up).astype(jnp.int32).astype(jnp.int16)
        gsend[d, :, at] = top * (1.0 / 32767.0)
        if d:
            net.send(("c", d, n), cq.at[d, n], half_chunk(q_out, z, n), me.dev(z=zz))

    def finish_step(k, n):
        for d in ((0,), (1, 3), (2,))[k]:
            finish(d, n)

    def total():
        own = [pltpu.make_async_copy(cq.at[0, n], half_chunk(q_out, z, n), local_sem.at[n]) for n in (0, 1)]
        for copy in own:
            copy.start()
        for d, dy in around:
            net.send(("t", d, dy), ts.at[mine], ts.at[mine], me.dev(x=(x + d) % 4, yl=(yl + dy) % 2))
        for d, dy in around:
            xx, yy = (x - d + 4) % 4, (yl + dy) % 2
            net.wait(("t", d, dy), ts.at[yy * 4 + xx], me.dev(x=xx, yl=yy))
        whole = ((ts[0] + ts[1]) + (ts[2] + ts[3])) + ((ts[4] + ts[5]) + (ts[6] + ts[7]))
        scale = (rows * 32) / whole
        for d in range(4):
            gsend[d, :, wide:] = scale
        gs[z] = gsend[0]
        for d in (1, 3, 2):
            net.send(("s", d), gsend.at[d], gs.at[z], me.dev(z=(z + d) % 4))
        for copy in own:
            copy.wait()
        for d in (1, 3, 2):
            src = (z - d + 4) % 4
            net.wait(("s", d), gs.at[src], me.dev(z=src))
        gs_out[...] = gs[...]
        for d in (1, 3, 2):
            src = (z - d + 4) % 4
            for n in (0, 1):
                net.wait(("c", d, n), half_chunk(q_out, src, n), me.dev(z=src))
        net.drain()

    steps = {"start": start, "mx": masses_x, "inv": masses_z, "own": own_a, "nb0": own_b, "z1": take_z1, "zo": opposite_z1,
             "tot": total, "home": home, "f": forward_x, "lx": raw_x, "sy": send_y, "sb": send_b, "sa": send_z0,
             "g": forward_z0, "y": take_y, "fin": finish_z0, "r": take_rest, "E": early, "C": finish_step,
             "L": lambda j, n: late(j, n, 0, 3), "O": lambda j, n: late(j, n, 3, 1)}
    for name, *which in ORDER:
        steps[name](*which)


def body(flow, pattern, keep):
    rows, cols = flow.shape
    tile = cols // pattern.shape[1]
    wide = cols // 4
    side = wide // 2
    vmem = pl.BlockSpec(memory_space=pltpu.VMEM)
    anyspace = pl.BlockSpec(memory_space=pl.ANY)
    messages = 152
    coded, factors = pl.pallas_call(
        lambda *refs: kernel(tile, *refs),
        out_shape=(jax.ShapeDtypeStruct((rows, cols), jnp.int16), jax.ShapeDtypeStruct((4, 1, 2 * wide), F32)),
        in_specs=[pl.BlockSpec(memory_space=pltpu.HBM)] * 3,
        out_specs=(anyspace, vmem),
        scratch_shapes=[
            pltpu.VMEM((rows, cols), BF16),
            pltpu.SMEM(pattern.shape, jnp.int32),
            pltpu.SMEM(keep.shape, jnp.int32),
            pltpu.VMEM((4, 4 * rows, cols), BF16),
            pltpu.VMEM((2, 32 * rows, side), BF16),
            pltpu.VMEM((rows, cols), BF16),
            pltpu.VMEM((3, rows, cols), BF16),
            pltpu.VMEM((rows, cols), BF16),
            pltpu.VMEM((3, 2, rows, side), BF16),
            pltpu.VMEM((2, rows, side), BF16),
            pltpu.VMEM((4 * rows, wide), F32),
            pltpu.VMEM((4, 2, rows, side), jnp.int16),
            pltpu.VMEM((4, 1, cols), F32),
            pltpu.VMEM((8, 1, cols), F32),
            pltpu.VMEM((2, 1, cols), F32),
            pltpu.VMEM((8, cols), F32),
            pltpu.VMEM((4, 8, wide), F32),
            pltpu.VMEM((8, 1, wide), F32),
            pltpu.VMEM((4, 1, 2 * wide), F32),
            pltpu.VMEM((4, 1, 2 * wide), F32),
            pltpu.SemaphoreType.DMA((messages,)),
            pltpu.SemaphoreType.DMA((messages,)),
            pltpu.SemaphoreType.DMA((3,)),
        ],
        compiler_params=pltpu.CompilerParams(
            collective_id=0, has_side_effects=True, vmem_limit_bytes=52000 * 1024),
        name="cluster",
    )(*(pltpu.with_memory_space_constraint(v, pltpu.HBM) for v in (flow, pattern, keep)))
    down = factors[:, 0, :wide].reshape(1, cols)
    scale = factors[:, 0, wide:].reshape(1, cols)
    expanded = coded.astype(F32) * down
    return expanded * expanded * scale


def solution(mesh):
    return jax.shard_map(
        body,
        mesh=mesh,
        in_specs=(P("row", "col"), P("row", "col"), P("row", "col")),
        out_specs=P("row", "col"),
        check_vma=False,
    )
```
